512 devices in a mesh: dp: 8 (over y_hi, core), expert: 64 (over z, x, y_lo).
Axes of the slice: x: 4, y: 8 (y_hi: 4, y_lo: 2; y = y_hi * 2 + y_lo), z: 8, core: 2. Of those that a mesh axis runs over, the one named last changes fastest.
Arguments:
- tokens: bfloat16 [65536, 3584], P(('dp', 'expert')), may hold values from -6 to 6
- cotangent: bfloat16 [65536, 3584], P(('dp', 'expert')), may hold values from -0.59765625 to 0.59765625
- route_ids: int32 [65536, 8], P(('dp', 'expert')), may hold values from 0 to 383, as said below
- gates: bfloat16 [65536, 8], P(('dp', 'expert')), may hold values from 0.099609375 to 1
- w_gate: bfloat16 [64, 3584, 128], P('expert', None, 'dp'), may hold values from -0.09375 to 0.09375
- w_up: bfloat16 [64, 3584, 128], P('expert', None, 'dp'), may hold values from -0.09375 to 0.09375
- w_down: bfloat16 [64, 3584, 128], P('expert', None, 'dp'), may hold values from -0.125 to 0.125
Outputs:
- relaid_gate: bfloat16 [64, 3584, 128], P('expert', 'dp')
- relaid_up: bfloat16 [64, 3584, 128], P('expert', 'dp')
- relaid_down: bfloat16 [64, 3584, 128], P('expert', 'dp')
- grad_gate: float32 [64, 3584, 128], P('expert', 'dp')
- grad_up: float32 [64, 3584, 128], P('expert', 'dp')
- grad_down: float32 [64, 3584, 128], P('expert', 'dp')
- token_grad: bfloat16 [65536, 3584], P(('dp', 'expert'))
- gate_grad: float32 [65536, 8], P(('dp', 'expert'))
The draws below stay inside these ranges and needn't reach their ends.
Inputs may be any that keep to these rules, and one draw needn't show every extreme that they name: `route_ids`: each row names 8 different experts. Among the 128 rows of one device, at most 6 routes name any one expert below 4; on every device of one index of dp, one same expert below 4 is named by exactly 6 routes.
All inputs are finite; a program needn't handle non-finite values.
Results may differ from the reference program's by a relative error of at most 0.02.
Values may be sent and summed in bfloat16 or wider, within the bound.
No kernel may reach another device: no remote copies, remote signals or barrier semaphores. Data moves between devices by JAX's collectives and lax.ppermute only.
A program may use at most 128 MiB of HBM per device.

```python
import jax
import jax.numpy as jnp
from jax import lax

D = 3584
HID = 2048
ALL_EXP = 384
TOPK = 8
HSPLIT = 16
CAP = 6
TOK_DEV = 128
HDEV = 128
SLABS = 64
EXPERTS = 4
TOKENS = 65536
N_DP = 8


def draw_route_ids(key, part):
    blocks = TOKENS // TOK_DEV
    rows_dp = blocks // SLABS
    subkeys = jax.random.split(key, 6)
    hot_row = jax.random.randint(subkeys[0], (rows_dp,), 0, EXPERTS)
    hot_expert = jnp.repeat(hot_row, SLABS)
    counts = jax.random.randint(subkeys[1], (blocks, EXPERTS), 0, CAP // 2 + 2)
    counts = jnp.where(jnp.arange(EXPERTS)[None, :] == hot_expert[:, None], CAP, counts)
    shuffle_keys = jax.random.split(subkeys[2], blocks * EXPERTS)
    shuffles = jax.vmap(lambda one_key: jax.random.permutation(one_key, TOK_DEV))(shuffle_keys)
    token_rank = jnp.argsort(shuffles, axis=1).reshape(blocks, EXPERTS, TOK_DEV)
    member = (token_rank < counts[:, :, None]).astype(jnp.int32)
    member = jnp.transpose(member, (0, 2, 1))
    position = jnp.cumsum(member, axis=2) - member
    count_slab = jnp.sum(member, axis=2)
    columns = jnp.arange(TOPK)
    expert_numbers = jnp.arange(EXPERTS)
    slab_pick = jnp.sum(member[:, :, None, :] * (position[:, :, None, :] == columns[None, None, :, None]) * expert_numbers[None, None, None, :], axis=3)
    outside_span = ALL_EXP - EXPERTS
    offset = jax.random.randint(subkeys[3], (blocks, TOK_DEV), 0, outside_span)
    stride = jax.random.randint(subkeys[4], (blocks, TOK_DEV), 1, outside_span // TOPK + 1)
    outside = EXPERTS + (offset[:, :, None] + (columns[None, None, :] - count_slab[:, :, None]) * stride[:, :, None]) % outside_span
    chosen = jnp.where(columns[None, None, :] < count_slab[:, :, None], slab_pick, outside)
    rotation = jax.random.randint(subkeys[5], (blocks, TOK_DEV, 1), 0, TOPK)
    chosen = jnp.take_along_axis(chosen, (columns[None, None, :] + rotation) % TOPK, axis=2)
    return chosen.reshape(TOKENS, TOPK).astype(jnp.int32)


def steps_of(rng, dims, cuts, low, top_value):
    factor_of = 1.0
    for dim, blocks in cuts:
        draws = jax.random.uniform(jax.random.fold_in(jax.random.fold_in(rng, 6), dim), (blocks,), jnp.float32, low / len(cuts), top_value / len(cuts))
        factor_of = factor_of * jnp.repeat(jnp.exp(draws), dims[dim] // blocks).reshape((-1,) + (1,) * (len(dims) - 1 - dim))
    return factor_of


def centred(rng, extent, width, reach, cuts=(), kind=jnp.bfloat16):
    entries = width * jax.random.normal(rng, extent, jnp.float32)
    if cuts:
        entries = entries * steps_of(rng, extent, cuts, -0.22, 0.18)
    return jnp.clip(entries, -reach, reach).astype(kind)


def setup_inputs(seed: int = 0) -> dict:
    key_of = jax.random.split(jax.random.key(seed), 8)
    tokens = centred(key_of[0], (TOKENS, D), 1.0, 6.0, ((0, 512),))
    cotangent = centred(key_of[1], (TOKENS, D), 0.1, 0.59765625, ((0, 512),))
    route_ids = draw_route_ids(jax.random.fold_in(key_of[7], 71), 0)
    gates = jnp.clip(0.099609375 + 0.9003906 * jax.random.uniform(key_of[3], (TOKENS, TOPK), jnp.float32) ** steps_of(key_of[3], (TOKENS, TOPK), ((0, 512),), -0.2, 0.2), 0.099609375, 1.0).astype(jnp.bfloat16)
    w_gate = centred(key_of[4], (SLABS, D, HDEV), D ** -0.5, 0.09375, ((0, 64), (2, 8)))
    w_up = centred(key_of[5], (SLABS, D, HDEV), D ** -0.5, 0.09375, ((0, 64), (2, 8)))
    w_down = centred(key_of[6], (SLABS, D, HDEV), HID ** -0.5, 0.125, ((0, 64), (2, 8)))
    return dict(tokens=tokens, cotangent=cotangent, route_ids=route_ids, gates=gates, w_gate=w_gate, w_up=w_up, w_down=w_down)


def reference(tokens, cotangent, route_ids, gates, w_gate, w_up, w_down):
    blocks = TOKENS // TOK_DEV
    route_count = TOK_DEV * TOPK
    slot_total = EXPERTS * CAP
    flat_ids = route_ids.reshape(blocks, route_count)
    expert_hits = (flat_ids[:, :, None] == jnp.arange(EXPERTS, dtype=jnp.int32)[None, None, :]).astype(jnp.int32)
    earlier = jnp.cumsum(expert_hits, axis=1) - expert_hits
    slot_rank = jnp.sum(earlier * expert_hits, axis=2)
    in_slab = jnp.sum(expert_hits, axis=2) > 0
    slot_index = flat_ids * CAP + slot_rank
    table = (slot_index[:, :, None] == jnp.arange(slot_total, dtype=jnp.int32)[None, None, :]) & in_slab[:, :, None]
    route_token = jnp.arange(route_count, dtype=jnp.int32) // TOPK
    slot_token = jnp.sum(jnp.where(table, route_token[None, :, None], 0), axis=1).astype(jnp.int32)
    slot_live = jnp.any(table, axis=1)
    global_token = (slot_token + (jnp.arange(blocks, dtype=jnp.int32) * TOK_DEV)[:, None]).astype(jnp.int32)
    gate_flat = gates.reshape(blocks, route_count)[:, :, None].astype(jnp.float32)
    gate_slots = jnp.sum(jnp.where(table, gate_flat, 0.0), axis=1).astype(jnp.bfloat16)
    token_slots = jnp.where(slot_live[:, :, None], tokens[global_token], jnp.zeros((), tokens.dtype))
    cotan_slots = jnp.where(slot_live[:, :, None], cotangent[global_token], jnp.zeros((), cotangent.dtype))

    def by_expert(values):
        shaped = values.reshape((blocks, EXPERTS, CAP) + values.shape[2:])
        moved = jnp.moveaxis(shaped, 1, 0)
        return moved.reshape((EXPERTS, N_DP, SLABS * CAP) + values.shape[2:])

    expert_tokens = by_expert(token_slots)
    expert_cotan = by_expert(cotan_slots)
    expert_gates = by_expert(gate_slots)

    def dp_partial(left, right):
        summed = jnp.einsum("ird,irh->idh", left.astype(jnp.float32), right.astype(jnp.float32))
        rounded = lax.optimization_barrier(summed.astype(jnp.bfloat16))
        return jnp.sum(rounded.astype(jnp.float32), axis=0)

    def expert_work(operands):
        index, x_three, dy_three, g_two = operands
        slot_x = x_three.reshape(-1, D)
        slot_dy = dy_three.reshape(-1, D)
        slot_g = g_two.reshape(-1).astype(jnp.float32)[:, None]
        part_total = jnp.zeros((slot_x.shape[0], D), jnp.float32)
        score_total = jnp.zeros((slot_x.shape[0],), jnp.float32)
        grads_gate, grads_up, grads_down = [], [], []
        for block in range(HSPLIT):
            slab = index * HSPLIT + block
            gate_w = lax.dynamic_index_in_dim(w_gate, slab, 0, keepdims=False)
            up_w = lax.dynamic_index_in_dim(w_up, slab, 0, keepdims=False)
            down_w = lax.dynamic_index_in_dim(w_down, slab, 0, keepdims=False)
            pre_gate = jnp.dot(slot_x, gate_w, preferred_element_type=jnp.float32)
            pre_up = jnp.dot(slot_x, up_w, preferred_element_type=jnp.float32)
            sigmoid_gate = jax.nn.sigmoid(pre_gate)
            activation = pre_gate * sigmoid_gate
            hidden = (activation * pre_up).astype(jnp.bfloat16)
            back_proj = jnp.dot(slot_dy, down_w, preferred_element_type=jnp.float32)
            score_part = jnp.sum(hidden.astype(jnp.float32) * back_proj, axis=1).astype(jnp.bfloat16)
            scaled = slot_g * back_proj
            d_gate = (scaled * pre_up * sigmoid_gate * (1.0 + pre_gate * (1.0 - sigmoid_gate))).astype(jnp.bfloat16)
            d_up = (scaled * activation).astype(jnp.bfloat16)
            hidden_gated = (slot_g * hidden.astype(jnp.float32)).astype(jnp.bfloat16)
            partial_value = (jnp.dot(d_gate, gate_w.T, preferred_element_type=jnp.float32)
                       + jnp.dot(d_up, up_w.T, preferred_element_type=jnp.float32)).astype(jnp.bfloat16)
            part_total = part_total + partial_value.astype(jnp.float32)
            score_total = score_total + score_part.astype(jnp.float32)
            grads_gate.append(dp_partial(x_three, d_gate.reshape(N_DP, -1, HDEV)))
            grads_up.append(dp_partial(x_three, d_up.reshape(N_DP, -1, HDEV)))
            grads_down.append(dp_partial(dy_three, hidden_gated.reshape(N_DP, -1, HDEV)))
        return part_total, score_total, jnp.stack(grads_gate), jnp.stack(grads_up), jnp.stack(grads_down)

    parts, scores, grad_gate, grad_up, grad_down = lax.map(
        expert_work, (jnp.arange(EXPERTS, dtype=jnp.int32), expert_tokens, expert_cotan, expert_gates))
    grad_gate = grad_gate.reshape(SLABS, D, HDEV)
    grad_up = grad_up.reshape(SLABS, D, HDEV)
    grad_down = grad_down.reshape(SLABS, D, HDEV)
    parts_blocks = jnp.moveaxis(parts.reshape(EXPERTS, blocks, CAP, D), 0, 1).reshape(blocks, slot_total, D)
    scores_blocks = jnp.moveaxis(scores.reshape(EXPERTS, blocks, CAP), 0, 1).reshape(blocks, slot_total)
    live_parts = jnp.where(slot_live[:, :, None], parts_blocks, 0.0)
    token_grad = jnp.zeros((TOKENS, D), jnp.float32).at[global_token.reshape(-1)].add(live_parts.reshape(-1, D))
    gate_grad = jnp.einsum("brc,bc->br", table.astype(jnp.float32), scores_blocks, precision=lax.Precision.HIGHEST)
    return (w_gate, w_up, w_down, grad_gate, grad_up, grad_down,
            token_grad.astype(jnp.bfloat16), gate_grad.reshape(TOKENS, TOPK))
```

```python
import jax
import jax.numpy as jnp
from jax import lax
from jax.sharding import Mesh
from jax.sharding import PartitionSpec as P

HSPLIT = 16
CAP = 6
PAD = 8
EXPERTS = 4
LANES = 128
DP = ("yh", "core")
COLOR_A = ("zl", "yl", "x")
BF = jnp.bfloat16
F32 = jnp.float32


def spread(block, axes):
    count = lax.axis_size(axes)
    copies = jnp.broadcast_to(block[None], (count,) + block.shape)
    got = lax.all_to_all(copies, axes, split_axis=0, concat_axis=0, tiled=True)
    return got.reshape((count * block.shape[0],) + block.shape[1:])


def dot(eq, a, b):
    return jnp.einsum(eq, a, b, preferred_element_type=F32)


def shards(tokens, cotangent, route_ids, gates, w_gate, w_up, w_down):
    tok_count, features = tokens.shape
    hidden_dev = w_gate.shape[2]

    mine = jnp.concatenate([w_gate[0].T, w_up[0].T, w_down[0].T], axis=0)
    gathered = lax.all_gather(mine, DP, axis=0, tiled=True)
    n_dp = lax.axis_size(DP)
    gathered = gathered.reshape(n_dp, 3, hidden_dev, features)

    ids = route_ids.T
    gates_t = gates.T.astype(F32)
    experts = jnp.arange(EXPERTS, dtype=jnp.int32)
    hits = ids[None] == experts[:, None, None]
    token_hit = jnp.any(hits, axis=1)
    before = (
        jnp.arange(tok_count)[:, None] < jnp.arange(tok_count)[None, :]
    ).astype(BF)
    rank = dot("et,tu->eu", token_hit.astype(BF), before)
    slots = jnp.arange(PAD, dtype=jnp.int32)
    pick = token_hit[:, None, :] & (rank.astype(jnp.int32)[:, None, :] == slots[None, :, None])
    gate_of = jnp.sum(jnp.where(hits, gates_t[None], 0.0), axis=1)
    gate_slots = jnp.sum(jnp.where(pick, gate_of[:, None, :], 0.0), axis=2)
    pick_rows = pick.reshape(EXPERTS * PAD, tok_count).astype(BF)
    tok_slots = dot("ct,td->cd", pick_rows, tokens).astype(BF)
    cot_slots = dot("ct,td->cd", pick_rows, cotangent).astype(BF)
    gate_cols = jnp.broadcast_to(gate_slots.astype(BF).reshape(-1, 1), (EXPERTS * PAD, LANES))
    rows = jnp.concatenate([tok_slots, gate_cols, cot_slots], axis=1)
    rows = rows.reshape(EXPERTS, PAD, -1)
    rows = lax.all_to_all(rows, "ex", split_axis=0, concat_axis=0, tiled=True)
    rows = rows.reshape(EXPERTS * PAD, -1)
    kept = jnp.arange(EXPERTS * CAP)
    keep = (
        (kept // CAP * PAD + kept % CAP)[:, None] == jnp.arange(EXPERTS * PAD)[None, :]
    ).astype(BF)
    wide = features + LANES
    tok_rows = dot("kc,cd->kd", keep, rows[:, :wide]).astype(BF)
    cot_rows = dot("kc,cd->kd", keep, rows[:, wide:]).astype(BF)

    tok_half = spread(tok_rows, "x")
    cot_half = spread(cot_rows, ("zl", "yl"))
    slot_all = spread(tok_half, ("zl", "yl"))
    slot_cotan = spread(cot_half, "x")
    slot_tokens = slot_all[:, :features]
    slot_gates = slot_all[:, features : features + 1].astype(F32)

    block = EXPERTS * CAP

    def to_tok_order(values):
        v = values.reshape(4, 4, block, values.shape[-1])
        return jnp.swapaxes(v, 0, 1).reshape(values.shape)

    slab = [gathered[:, j].reshape(n_dp * hidden_dev, features) for j in range(3)]
    gate_slab, up_slab, down_slab = slab
    pre_gate = dot("rd,hd->rh", slot_tokens, gate_slab)
    pre_up = dot("rd,hd->rh", slot_tokens, up_slab)
    sigmoid_gate = jax.nn.sigmoid(pre_gate)
    activation = pre_gate * sigmoid_gate
    hidden = (activation * pre_up).astype(BF)
    back_proj = to_tok_order(dot("rd,hd->rh", slot_cotan, down_slab))
    score = jnp.sum(hidden.astype(F32) * back_proj, axis=1, keepdims=True).astype(BF)
    scaled = slot_gates * back_proj
    d_gate = (scaled * pre_up * sigmoid_gate * (1.0 + pre_gate * (1.0 - sigmoid_gate))).astype(BF)
    d_up = (scaled * activation).astype(BF)
    hidden_gated = to_tok_order((slot_gates * hidden.astype(F32)).astype(BF))

    grads = jnp.stack(
        [
            dot("rd,rh->dh", slot_tokens, d_gate).astype(BF).reshape(n_dp, -1, LANES),
            dot("rd,rh->dh", slot_tokens, d_up).astype(BF).reshape(n_dp, -1, LANES),
            dot("rd,rh->dh", slot_cotan, hidden_gated).astype(BF).reshape(n_dp, -1, LANES),
        ],
        axis=1,
    )
    grads = lax.psum_scatter(grads, DP, scatter_dimension=0, tiled=True)[0].astype(F32)

    partial = (
        dot("rh,hd->rd", d_gate, gate_slab) + dot("rh,hd->rd", d_up, up_slab)
    ).astype(BF)
    back = jnp.concatenate([partial, jnp.broadcast_to(score, (score.shape[0], LANES))], axis=1)
    back = back.reshape(HSPLIT, block, -1)
    back = lax.all_to_all(back, COLOR_A, split_axis=0, concat_axis=0, tiled=True)
    back = back.reshape(HSPLIT * block, -1)
    fold = jnp.tile(keep.T, (1, HSPLIT))
    summed = dot("ck,kd->cd", fold, back)
    score_sum = summed[:, features:]
    high = lax.reduce_precision(score_sum, 8, 7)
    lane = jnp.arange(LANES)[None, :]
    score_cols = jnp.where(lane < LANES // 2, high, score_sum - high)
    home = jnp.concatenate([summed[:, :features], score_cols], axis=1).astype(BF)
    home = lax.all_to_all(
        home.reshape(EXPERTS, PAD, -1), "ex", split_axis=0, concat_axis=0, tiled=True
    ).reshape(EXPERTS * PAD, -1)
    token_grad = dot("ct,cd->td", pick_rows, home[:, :features]).astype(BF)
    pair = home[:, features:].astype(F32)
    score_slots = (pair[:, :1] + pair[:, LANES // 2 : LANES // 2 + 1]).reshape(EXPERTS, PAD, 1)
    score_token = jnp.sum(jnp.where(pick, score_slots, 0.0), axis=1)
    gate_grad = jnp.sum(jnp.where(hits, score_token[:, None, :], 0.0), axis=0).T

    start = lax.axis_index(DP) * (features // n_dp)
    relaid = [
        lax.dynamic_slice_in_dim(w, start, features // n_dp, axis=1).T[None] for w in slab
    ]
    return (*relaid, grads[0:1], grads[1:2], grads[2:3], token_grad, gate_grad)


def solution(mesh):
    fine = Mesh(
        mesh.devices.reshape(4, 2, 4, 2, 4, 2), ("yh", "core", "ex", "zl", "x", "yl")
    )
    expert = ("ex", "zl", "x", "yl")
    rows = P(DP + expert, None)
    weights = P(expert, None, DP)
    laid = P(expert, DP, None)
    return jax.shard_map(
        shards,
        mesh=fine,
        in_specs=(rows,) * 4 + (weights,) * 3,
        out_specs=(laid,) * 6 + (rows,) * 2,
        check_vma=False,
    )
```

```python
import jax
import jax.numpy as jnp
from jax import lax
from jax.sharding import Mesh
from jax.sharding import PartitionSpec as P

HSPLIT = 16
CAP = 6
PAD = 8
EXPERTS = 4
LANES = 128
DP = ("yh", "core")
COLOR_A = ("zl", "yl", "x")
BF = jnp.bfloat16
F32 = jnp.float32


def spread(block, axes):
    count = lax.axis_size(axes)
    copies = jnp.broadcast_to(block[None], (count,) + block.shape)
    got = lax.all_to_all(copies, axes, split_axis=0, concat_axis=0, tiled=True)
    return got.reshape((count * block.shape[0],) + block.shape[1:])


def put(total, block, at):
    return lax.dynamic_update_slice_in_dim(total, block[None], at, axis=0)


def spread_square(block):
    z, y = lax.axis_index("zl"), lax.axis_index("yl")
    me = 2 * z + y
    total = put(jnp.zeros((4,) + block.shape, block.dtype), block, me)
    for off in (1, 2, 3):
        got = lax.ppermute(block, ("zl", "yl"), [(i, i ^ off) for i in range(4)])
        total = put(total, got, me ^ off)
    return total.reshape((4 * block.shape[0],) + block.shape[1:])


RIGHT = [(i, (i + 1) % 4) for i in range(4)]
LEFT = [(i, (i + 3) % 4) for i in range(4)]


def spread_ring(block):
    me = lax.axis_index("x")
    half = block.shape[0] // 2
    from_left = lax.ppermute(block, "x", RIGHT)
    from_right = lax.ppermute(block, "x", LEFT)
    far_top = lax.ppermute(from_left[:half], "x", RIGHT)
    far_low = lax.ppermute(from_right[half:], "x", LEFT)
    total = put(jnp.zeros((4,) + block.shape, block.dtype), block, me)
    total = put(total, from_left, (me + 3) % 4)
    total = put(total, from_right, (me + 1) % 4)
    far = (me + 2) % 4
    total = lax.dynamic_update_slice(total, far_top[None], (far, 0, 0))
    total = lax.dynamic_update_slice(total, far_low[None], (far, half, 0))
    return total.reshape((4 * block.shape[0],) + block.shape[1:])


def dot(eq, a, b):
    return jnp.einsum(eq, a, b, preferred_element_type=F32)


def shards(tokens, cotangent, route_ids, gates, w_gate, w_up, w_down):
    tok_count, features = tokens.shape
    hidden_dev = w_gate.shape[2]

    mine = jnp.concatenate([w_gate[0].T, w_up[0].T, w_down[0].T], axis=0)
    gathered = lax.all_gather(mine, DP, axis=0, tiled=True)
    n_dp = lax.axis_size(DP)
    gathered = gathered.reshape(n_dp, 3, hidden_dev, features)

    ids = route_ids.T
    gates_t = gates.T.astype(F32)
    experts = jnp.arange(EXPERTS, dtype=jnp.int32)
    hits = ids[None] == experts[:, None, None]
    token_hit = jnp.any(hits, axis=1)
    before = (
        jnp.arange(tok_count)[:, None] < jnp.arange(tok_count)[None, :]
    ).astype(BF)
    rank = dot("et,tu->eu", token_hit.astype(BF), before)
    slots = jnp.arange(PAD, dtype=jnp.int32)
    pick = token_hit[:, None, :] & (rank.astype(jnp.int32)[:, None, :] == slots[None, :, None])
    gate_of = jnp.sum(jnp.where(hits, gates_t[None], 0.0), axis=1)
    gate_slots = jnp.sum(jnp.where(pick, gate_of[:, None, :], 0.0), axis=2)
    pick_rows = pick.reshape(EXPERTS * PAD, tok_count).astype(BF)
    tok_slots = dot("ct,td->cd", pick_rows, tokens).astype(BF)
    cot_slots = dot("ct,td->cd", pick_rows, cotangent).astype(BF)
    gate_cols = jnp.broadcast_to(gate_slots.astype(BF).reshape(-1, 1), (EXPERTS * PAD, LANES))
    rows = jnp.concatenate([tok_slots, gate_cols, cot_slots], axis=1)
    rows = rows.reshape(EXPERTS, PAD, -1)
    rows = lax.all_to_all(rows, "ex", split_axis=0, concat_axis=0, tiled=True)
    rows = rows.reshape(EXPERTS * PAD, -1)
    kept = jnp.arange(EXPERTS * CAP)
    keep = (
        (kept // CAP * PAD + kept % CAP)[:, None] == jnp.arange(EXPERTS * PAD)[None, :]
    ).astype(BF)
    wide = features + LANES
    tok_rows = dot("kc,cd->kd", keep, rows[:, :wide]).astype(BF)
    cot_rows = dot("kc,cd->kd", keep, rows[:, wide:]).astype(BF)

    tok_half = spread(tok_rows, "x")
    cot_half = spread_square(cot_rows)
    tok_half, cot_half, gathered = lax.optimization_barrier((tok_half, cot_half, gathered))
    slot_all = spread(tok_half, ("zl", "yl"))
    slot_cotan = spread_ring(cot_half)
    slot_tokens = slot_all[:, :features]
    slot_gates = slot_all[:, features : features + 1].astype(F32)

    block = EXPERTS * CAP

    def to_tok_order(values):
        v = values.reshape(4, 4, block, values.shape[-1])
        return jnp.swapaxes(v, 0, 1).reshape(values.shape)

    slab = [gathered[:, j].reshape(n_dp * hidden_dev, features) for j in range(3)]
    gate_slab, up_slab, down_slab = slab
    pre_gate = dot("rd,hd->rh", slot_tokens, gate_slab)
    pre_up = dot("rd,hd->rh", slot_tokens, up_slab)
    sigmoid_gate = jax.nn.sigmoid(pre_gate)
    activation = pre_gate * sigmoid_gate
    hidden = (activation * pre_up).astype(BF)
    back_proj = to_tok_order(dot("rd,hd->rh", slot_cotan, down_slab))
    score = jnp.sum(hidden.astype(F32) * back_proj, axis=1, keepdims=True).astype(BF)
    scaled = slot_gates * back_proj
    d_gate = (scaled * pre_up * sigmoid_gate * (1.0 + pre_gate * (1.0 - sigmoid_gate))).astype(BF)
    d_up = (scaled * activation).astype(BF)
    hidden_gated = to_tok_order((slot_gates * hidden.astype(F32)).astype(BF))

    grads = jnp.stack(
        [
            dot("rd,rh->dh", slot_tokens, d_gate).astype(BF).reshape(n_dp, -1, LANES),
            dot("rd,rh->dh", slot_tokens, d_up).astype(BF).reshape(n_dp, -1, LANES),
            dot("rd,rh->dh", slot_cotan, hidden_gated).astype(BF).reshape(n_dp, -1, LANES),
        ],
        axis=1,
    )
    grads = lax.psum_scatter(grads, DP, scatter_dimension=0, tiled=True)[0].astype(F32)

    partial = (
        dot("rh,hd->rd", d_gate, gate_slab) + dot("rh,hd->rd", d_up, up_slab)
    ).astype(BF)
    back = jnp.concatenate([partial, jnp.broadcast_to(score, (score.shape[0], LANES))], axis=1)
    back = back.reshape(HSPLIT, block, -1)
    back = lax.all_to_all(back, COLOR_A, split_axis=0, concat_axis=0, tiled=True)
    back = back.reshape(HSPLIT * block, -1)
    fold = jnp.tile(keep.T, (1, HSPLIT))
    summed = dot("ck,kd->cd", fold, back)
    score_sum = summed[:, features:]
    high = lax.reduce_precision(score_sum, 8, 7)
    lane = jnp.arange(LANES)[None, :]
    score_cols = jnp.where(lane < LANES // 2, high, score_sum - high)
    home = jnp.concatenate([summed[:, :features], score_cols], axis=1).astype(BF)
    home = lax.all_to_all(
        home.reshape(EXPERTS, PAD, -1), "ex", split_axis=0, concat_axis=0, tiled=True
    ).reshape(EXPERTS * PAD, -1)
    token_grad = dot("ct,cd->td", pick_rows, home[:, :features]).astype(BF)
    pair = home[:, features:].astype(F32)
    score_slots = (pair[:, :1] + pair[:, LANES // 2 : LANES // 2 + 1]).reshape(EXPERTS, PAD, 1)
    score_token = jnp.sum(jnp.where(pick, score_slots, 0.0), axis=1)
    gate_grad = jnp.sum(jnp.where(hits, score_token[:, None, :], 0.0), axis=0).T

    start = lax.axis_index(DP) * (features // n_dp)
    relaid = [
        lax.dynamic_slice_in_dim(w, start, features // n_dp, axis=1).T[None] for w in slab
    ]
    return (*relaid, grads[0:1], grads[1:2], grads[2:3], token_grad, gate_grad)


def solution(mesh):
    fine = Mesh(
        mesh.devices.reshape(4, 2, 4, 2, 4, 2), ("yh", "core", "ex", "zl", "x", "yl")
    )
    expert = ("ex", "zl", "x", "yl")
    rows = P(DP + expert, None)
    weights = P(expert, None, DP)
    laid = P(expert, DP, None)
    return jax.shard_map(
        shards,
        mesh=fine,
        in_specs=(rows,) * 4 + (weights,) * 3,
        out_specs=(laid,) * 6 + (rows,) * 2,
        check_vma=False,
    )
```

```python
import jax
import jax.numpy as jnp
from jax import lax
from jax.sharding import Mesh
from jax.sharding import PartitionSpec as P

HSPLIT = 16
CAP = 6
PAD = 8
EXPERTS = 4
LANES = 128
DP = ("yh", "core")
BF = jnp.bfloat16
F32 = jnp.float32


def spread(block, axes):
    count = lax.axis_size(axes)
    copies = jnp.broadcast_to(block[None], (count,) + block.shape)
    got = lax.all_to_all(copies, axes, split_axis=0, concat_axis=0, tiled=True)
    return got.reshape((count * block.shape[0],) + block.shape[1:])


RIGHT = [(i, (i + 1) % 4) for i in range(4)]
LEFT = [(i, (i + 3) % 4) for i in range(4)]
SWAP = [(0, 1), (1, 0)]


def put(total, block, at, row=0):
    return lax.dynamic_update_slice(total, block[None], (at, row, 0))


def square_index():
    return 2 * lax.axis_index("zl") + lax.axis_index("yl")


def spread_direct(block):
    me = square_index()
    total = put(jnp.zeros((4,) + block.shape, block.dtype), block, me)
    for off in (1, 2, 3):
        got = lax.ppermute(block, ("zl", "yl"), [(i, i ^ off) for i in range(4)])
        total = put(total, got, me ^ off)
    return total


def spread_square(block, held):
    me = square_index()
    top, low = block[:2], block[2:]
    top_z = lax.ppermute(top, "zl", SWAP)
    low_y = lax.ppermute(low, "yl", SWAP)
    top_z, low_y, held = lax.optimization_barrier((top_z, low_y, held))
    top_two = lax.ppermute(jnp.stack([top, top_z]), "yl", SWAP)
    low_two = lax.ppermute(jnp.stack([low, low_y]), "zl", SWAP)
    total = jnp.zeros((block.shape[0], 4) + block.shape[1:], block.dtype)

    def place(total, piece, first, at):
        return lax.dynamic_update_slice(total, piece[:, None], (first, at, 0, 0))

    total = place(total, block, 0, me)
    total = place(total, top_z, 0, me ^ 2)
    total = place(total, low_y, 2, me ^ 1)
    total = place(total, top_two[0], 0, me ^ 1)
    total = place(total, top_two[1], 0, me ^ 3)
    total = place(total, low_two[0], 2, me ^ 2)
    total = place(total, low_two[1], 2, me ^ 3)
    return total, held


def spread_ring(block):
    me = lax.axis_index("x")
    half = block.shape[0] // 2
    from_left = lax.ppermute(block, "x", RIGHT)
    from_right = lax.ppermute(block, "x", LEFT)
    far_top = lax.ppermute(from_left[:half], "x", RIGHT)
    far_low = lax.ppermute(from_right[half:], "x", LEFT)
    total = put(jnp.zeros((4,) + block.shape, block.dtype), block, me)
    total = put(total, from_left, (me + 3) % 4)
    total = put(total, from_right, (me + 1) % 4)
    total = put(total, far_top, (me + 2) % 4)
    return put(total, far_low, (me + 2) % 4, half)


def sum_ring(parts):
    me = lax.axis_index("x")
    half = parts.shape[1] // 2

    def part(off):
        return lax.dynamic_index_in_dim(parts, (me + off) % 4, 0, keepdims=False)

    far = part(2)
    top = lax.ppermute(far[:half], "x", RIGHT)
    low = lax.ppermute(far[half:], "x", LEFT)
    right, left = part(1), part(3)
    right = jnp.concatenate([add(right[:half], top), right[half:]], axis=0)
    left = jnp.concatenate([left[:half], add(left[half:], low)], axis=0)
    return part(0), lax.ppermute(right, "x", RIGHT), lax.ppermute(left, "x", LEFT)


def add(a, b):
    return (a.astype(F32) + b.astype(F32)).astype(BF)


def dot(eq, a, b):
    return jnp.einsum(eq, a, b, preferred_element_type=F32)


def shards(tokens, cotangent, route_ids, gates, w_gate, w_up, w_down):
    tok_count, features = tokens.shape
    hidden_dev = w_gate.shape[2]

    mine = jnp.concatenate([w_gate[0].T, w_up[0].T, w_down[0].T], axis=0)
    gathered = lax.all_gather(mine, DP, axis=0, tiled=True)
    n_dp = lax.axis_size(DP)

    ids = route_ids.T
    gates_t = gates.T.astype(F32)
    experts = jnp.arange(EXPERTS, dtype=jnp.int32)
    hits = ids[None] == experts[:, None, None]
    token_hit = jnp.any(hits, axis=1)
    before = (
        jnp.arange(tok_count)[:, None] < jnp.arange(tok_count)[None, :]
    ).astype(BF)
    rank = dot("et,tu->eu", token_hit.astype(BF), before)
    slots = jnp.arange(PAD, dtype=jnp.int32)
    pick = token_hit[:, None, :] & (rank.astype(jnp.int32)[:, None, :] == slots[None, :, None])
    gate_of = jnp.sum(jnp.where(hits, gates_t[None], 0.0), axis=1)
    gate_slots = jnp.sum(jnp.where(pick, gate_of[:, None, :], 0.0), axis=2)
    pick_rows = pick.reshape(EXPERTS * PAD, tok_count).astype(BF)
    tok_slots = dot("ct,td->cd", pick_rows, tokens).astype(BF)
    cot_slots = dot("ct,td->cd", pick_rows, cotangent).astype(BF)
    gate_cols = jnp.broadcast_to(gate_slots.astype(BF).reshape(-1, 1), (EXPERTS * PAD, LANES))
    rows = jnp.concatenate([tok_slots, gate_cols, cot_slots], axis=1)
    rows = rows.reshape(EXPERTS, PAD, -1)
    rows = lax.all_to_all(rows, "ex", split_axis=0, concat_axis=0, tiled=True)
    rows = rows.reshape(EXPERTS * PAD, -1)
    kept = jnp.arange(EXPERTS * CAP)
    keep = (
        (kept // CAP * PAD + kept % CAP)[:, None] == jnp.arange(EXPERTS * PAD)[None, :]
    ).astype(BF)
    wide = features + LANES
    tok_rows = dot("kc,cd->kd", keep, rows[:, :wide]).astype(BF)
    cot_rows = dot("kc,cd->kd", keep, rows[:, wide:]).astype(BF)

    block = EXPERTS * CAP
    tok_half = spread(tok_rows, "x").reshape(4, block, wide)
    cot_half = spread_direct(cot_rows).reshape(4 * block, features)
    slot_all, gathered = spread_square(tok_half, gathered)
    slot_all = slot_all.reshape(-1, wide)
    slot_cotan = spread_ring(cot_half).reshape(-1, features)
    slot_tokens = slot_all[:, :features]
    slot_gates = slot_all[:, features : features + 1].astype(F32)
    gathered = gathered.reshape(n_dp, 3, hidden_dev, features)

    slab = [gathered[:, j].reshape(n_dp * hidden_dev, features) for j in range(3)]
    gate_slab, up_slab, down_slab = slab
    pre_gate = dot("rd,hd->rh", slot_tokens, gate_slab)
    pre_up = dot("rd,hd->rh", slot_tokens, up_slab)
    sigmoid_gate = jax.nn.sigmoid(pre_gate)
    activation = pre_gate * sigmoid_gate
    hidden = (activation * pre_up).astype(BF)
    back_proj = dot("rd,hd->rh", slot_cotan, down_slab)
    score = jnp.sum(hidden.astype(F32) * back_proj, axis=1, keepdims=True).astype(BF)
    scaled = slot_gates * back_proj
    d_gate = (scaled * pre_up * sigmoid_gate * (1.0 + pre_gate * (1.0 - sigmoid_gate))).astype(BF)
    d_up = (scaled * activation).astype(BF)
    hidden_gated = (slot_gates * hidden.astype(F32)).astype(BF)

    grads = jnp.stack(
        [
            dot("rd,rh->dh", slot_tokens, d_gate).astype(BF).reshape(n_dp, -1, LANES),
            dot("rd,rh->dh", slot_tokens, d_up).astype(BF).reshape(n_dp, -1, LANES),
            dot("rd,rh->dh", slot_cotan, hidden_gated).astype(BF).reshape(n_dp, -1, LANES),
        ],
        axis=1,
    )
    grads = lax.psum_scatter(grads, DP, scatter_dimension=0, tiled=True)[0].astype(F32)

    partial = (
        dot("rh,hd->rd", d_gate, gate_slab) + dot("rh,hd->rd", d_up, up_slab)
    ).astype(BF)
    back = jnp.concatenate([partial, jnp.broadcast_to(score, (score.shape[0], LANES))], axis=1)
    trio = jnp.concatenate(sum_ring(back.reshape(4, 4 * block, wide)), axis=0)
    row = jnp.arange(4 * block)
    target = (row // CAP % EXPERTS * 4 + row // block) * PAD + row % CAP
    fold = (jnp.arange(HSPLIT * PAD)[:, None] == target[None, :]).astype(BF)
    home = dot("ck,kd->cd", jnp.tile(fold, (1, 3)), trio).astype(BF)
    home = lax.all_to_all(
        home.reshape(HSPLIT, PAD, wide), ("ex", "zl", "yl"), split_axis=0, concat_axis=0, tiled=True
    ).reshape(HSPLIT * PAD, wide)
    pick_home = jnp.broadcast_to(pick[:, None], (EXPERTS, 4, PAD, tok_count))
    pick_home = pick_home.reshape(HSPLIT * PAD, tok_count).astype(BF)
    token_grad = dot("ct,cd->td", pick_home, home[:, :features]).astype(BF)
    score_slots = jnp.sum(
        home[:, features : features + 1].astype(F32).reshape(EXPERTS, 4, PAD, 1), axis=1
    )
    score_token = jnp.sum(jnp.where(pick, score_slots, 0.0), axis=1)
    gate_grad = jnp.sum(jnp.where(hits, score_token[:, None, :], 0.0), axis=0).T

    start = lax.axis_index(DP) * (features // n_dp)
    relaid = [
        lax.dynamic_slice_in_dim(w, start, features // n_dp, axis=1).T[None] for w in slab
    ]
    return (*relaid, grads[0:1], grads[1:2], grads[2:3], token_grad, gate_grad)


def solution(mesh):
    fine = Mesh(
        mesh.devices.reshape(4, 2, 4, 2, 4, 2), ("yh", "core", "ex", "zl", "x", "yl")
    )
    expert = ("ex", "zl", "x", "yl")
    rows = P(DP + expert, None)
    weights = P(expert, None, DP)
    laid = P(expert, DP, None)
    return jax.shard_map(
        shards,
        mesh=fine,
        in_specs=(rows,) * 4 + (weights,) * 3,
        out_specs=(laid,) * 6 + (rows,) * 2,
        check_vma=False,
    )
```

```python
import jax
import jax.numpy as jnp
from jax import lax
from jax.sharding import Mesh
from jax.sharding import PartitionSpec as P

HSPLIT = 16
CAP = 6
PAD = 8
EXPERTS = 4
LANES = 128
DP = ("yh", "core")
BF = jnp.bfloat16
F32 = jnp.float32


def spread(block, axes):
    count = lax.axis_size(axes)
    copies = jnp.broadcast_to(block[None], (count,) + block.shape)
    got = lax.all_to_all(copies, axes, split_axis=0, concat_axis=0, tiled=True)
    return got.reshape((count * block.shape[0],) + block.shape[1:])


def dot(eq, a, b):
    return jnp.einsum(eq, a, b, preferred_element_type=F32)


def shards(tokens, cotangent, route_ids, gates, w_gate, w_up, w_down):
    tok_count, features = tokens.shape
    hidden_dev = w_gate.shape[2]

    mine = jnp.concatenate([w_gate[0].T, w_up[0].T, w_down[0].T], axis=0)
    gathered = lax.all_gather(mine, DP, axis=0, tiled=True)
    n_dp = lax.axis_size(DP)

    ids = route_ids.T
    gates_t = gates.T.astype(F32)
    experts = jnp.arange(EXPERTS, dtype=jnp.int32)
    hits = ids[None] == experts[:, None, None]
    token_hit = jnp.any(hits, axis=1)
    before = (
        jnp.arange(tok_count)[:, None] < jnp.arange(tok_count)[None, :]
    ).astype(BF)
    rank = dot("et,tu->eu", token_hit.astype(BF), before)
    slots = jnp.arange(PAD, dtype=jnp.int32)
    pick = token_hit[:, None, :] & (rank.astype(jnp.int32)[:, None, :] == slots[None, :, None])
    gate_of = jnp.sum(jnp.where(hits, gates_t[None], 0.0), axis=1)
    gate_slots = jnp.sum(jnp.where(pick, gate_of[:, None, :], 0.0), axis=2)
    pick_rows = pick.reshape(EXPERTS * PAD, tok_count).astype(BF)
    tok_slots = dot("ct,td->cd", pick_rows, tokens).astype(BF)
    cot_slots = dot("ct,td->cd", pick_rows, cotangent).astype(BF)
    gate_cols = jnp.broadcast_to(gate_slots.astype(BF).reshape(-1, 1), (EXPERTS * PAD, LANES))
    rows = jnp.concatenate([tok_slots, gate_cols, cot_slots], axis=1)
    rows = rows.reshape(EXPERTS, PAD, -1)
    rows = lax.all_to_all(rows, "ex", split_axis=0, concat_axis=0, tiled=True)
    rows = rows.reshape(EXPERTS * PAD, -1)
    kept = jnp.arange(EXPERTS * CAP)
    keep = (
        (kept // CAP * PAD + kept % CAP)[:, None] == jnp.arange(EXPERTS * PAD)[None, :]
    ).astype(BF)
    wide = features + LANES
    tok_rows = dot("kc,cd->kd", keep, rows[:, :wide]).astype(BF)
    cot_rows = dot("kc,cd->kd", keep, rows[:, wide:]).astype(BF)

    block = EXPERTS * CAP
    tok_half = lax.all_gather(tok_rows, "x", axis=0, tiled=True)
    cot_half = lax.all_gather(cot_rows, ("zl", "yl"), axis=0, tiled=True)
    cot_half, gathered = lax.optimization_barrier((cot_half, gathered))
    slot_all = spread(tok_half, ("zl", "yl"))
    slot_cotan = lax.all_gather(cot_half, "x", axis=0, tiled=True)
    slot_tokens = slot_all[:, :features]
    gathered = gathered.reshape(n_dp, 3, hidden_dev, features)

    def reorder(values):
        v = values.reshape(4, 4, block, values.shape[-1])
        return jnp.swapaxes(v, 0, 1).reshape(values.shape)

    slab = [gathered[:, j].reshape(n_dp * hidden_dev, features) for j in range(3)]
    gate_slab, up_slab, down_slab = slab
    pre_gate = reorder(dot("rd,hd->rh", slot_tokens, gate_slab))
    pre_up = reorder(dot("rd,hd->rh", slot_tokens, up_slab))
    slot_gates = reorder(slot_all[:, features : features + 1]).astype(F32)
    sigmoid_gate = jax.nn.sigmoid(pre_gate)
    activation = pre_gate * sigmoid_gate
    hidden = (activation * pre_up).astype(BF)
    back_proj = dot("rd,hd->rh", slot_cotan, down_slab)
    score = jnp.sum(hidden.astype(F32) * back_proj, axis=1, keepdims=True).astype(BF)
    scaled = slot_gates * back_proj
    d_gate = (scaled * pre_up * sigmoid_gate * (1.0 + pre_gate * (1.0 - sigmoid_gate))).astype(BF)
    d_up = (scaled * activation).astype(BF)
    hidden_gated = (slot_gates * hidden.astype(F32)).astype(BF)

    grads = jnp.stack(
        [
            dot("rd,rh->dh", slot_tokens, reorder(d_gate)).astype(BF).reshape(n_dp, -1, LANES),
            dot("rd,rh->dh", slot_tokens, reorder(d_up)).astype(BF).reshape(n_dp, -1, LANES),
            dot("rd,rh->dh", slot_cotan, hidden_gated).astype(BF).reshape(n_dp, -1, LANES),
        ],
        axis=1,
    )
    grads = lax.psum_scatter(grads, DP, scatter_dimension=0, tiled=True)[0].astype(F32)

    partial = (
        dot("rh,hd->rd", d_gate, gate_slab) + dot("rh,hd->rd", d_up, up_slab)
    ).astype(BF)
    back = jnp.concatenate([partial, jnp.broadcast_to(score, (score.shape[0], LANES))], axis=1)
    back = back.reshape(8, 2 * block, wide)
    back = lax.all_to_all(back, ("x", "zl"), split_axis=0, concat_axis=0, tiled=True)
    back = back.reshape(HSPLIT * block, wide)
    row = jnp.arange(2 * block)
    target = (row // CAP % EXPERTS * 2 + row // block) * PAD + row % CAP
    fold = (jnp.arange(2 * EXPERTS * PAD)[:, None] == target[None, :]).astype(BF)
    home = dot("ck,kd->cd", jnp.tile(fold, (1, 8)), back).astype(BF)
    home = lax.all_to_all(
        home.reshape(2 * EXPERTS, PAD, wide), ("ex", "yl"), split_axis=0, concat_axis=0, tiled=True
    ).reshape(2 * EXPERTS * PAD, wide)
    pick_home = jnp.broadcast_to(pick[:, None], (EXPERTS, 2, PAD, tok_count))
    pick_home = pick_home.reshape(2 * EXPERTS * PAD, tok_count).astype(BF)
    token_grad = dot("ct,cd->td", pick_home, home[:, :features]).astype(BF)
    score_slots = jnp.sum(
        home[:, features : features + 1].astype(F32).reshape(EXPERTS, 2, PAD, 1), axis=1
    )
    score_token = jnp.sum(jnp.where(pick, score_slots, 0.0), axis=1)
    gate_grad = jnp.sum(jnp.where(hits, score_token[:, None, :], 0.0), axis=0).T

    start = lax.axis_index(DP) * (features // n_dp)
    relaid = [
        lax.dynamic_slice_in_dim(w, start, features // n_dp, axis=1).T[None] for w in slab
    ]
    return (*relaid, grads[0:1], grads[1:2], grads[2:3], token_grad, gate_grad)


def solution(mesh):
    fine = Mesh(
        mesh.devices.reshape(4, 2, 4, 2, 4, 2), ("yh", "core", "ex", "zl", "x", "yl")
    )
    expert = ("ex", "zl", "x", "yl")
    rows = P(DP + expert, None)
    weights = P(expert, None, DP)
    laid = P(expert, DP, None)
    return jax.shard_map(
        shards,
        mesh=fine,
        in_specs=(rows,) * 4 + (weights,) * 3,
        out_specs=(laid,) * 6 + (rows,) * 2,
        check_vma=False,
    )
```

```python
import jax
import jax.numpy as jnp
from jax import lax
from jax.sharding import Mesh
from jax.sharding import PartitionSpec as P

HSPLIT = 16
CAP = 6
PAD = 8
EXPERTS = 4
LANES = 128
DP = ("yh", "core")
BF = jnp.bfloat16
F32 = jnp.float32


def spread(block, axes):
    count = lax.axis_size(axes)
    copies = jnp.broadcast_to(block[None], (count,) + block.shape)
    got = lax.all_to_all(copies, axes, split_axis=0, concat_axis=0, tiled=True)
    return got.reshape((count * block.shape[0],) + block.shape[1:])


def dot(eq, a, b):
    return jnp.einsum(eq, a, b, preferred_element_type=F32)


def shards(tokens, cotangent, route_ids, gates, w_gate, w_up, w_down):
    tok_count, features = tokens.shape
    hidden_dev = w_gate.shape[2]

    mine = jnp.concatenate([w_gate[0].T, w_up[0].T, w_down[0].T], axis=0)
    gathered = lax.all_gather(mine, DP, axis=0, tiled=True)
    n_dp = lax.axis_size(DP)

    ids = route_ids.T
    gates_t = gates.T.astype(F32)
    experts = jnp.arange(EXPERTS, dtype=jnp.int32)
    hits = ids[None] == experts[:, None, None]
    token_hit = jnp.any(hits, axis=1)
    before = (
        jnp.arange(tok_count)[:, None] < jnp.arange(tok_count)[None, :]
    ).astype(BF)
    rank = dot("et,tu->eu", token_hit.astype(BF), before)
    slots = jnp.arange(PAD, dtype=jnp.int32)
    pick = token_hit[:, None, :] & (rank.astype(jnp.int32)[:, None, :] == slots[None, :, None])
    gate_of = jnp.sum(jnp.where(hits, gates_t[None], 0.0), axis=1)
    gate_slots = jnp.sum(jnp.where(pick, gate_of[:, None, :], 0.0), axis=2)
    pick_rows = pick.reshape(EXPERTS * PAD, tok_count).astype(BF)
    tok_slots = dot("ct,td->cd", pick_rows, tokens).astype(BF)
    cot_slots = dot("ct,td->cd", pick_rows, cotangent).astype(BF)
    gate_cols = jnp.broadcast_to(gate_slots.astype(BF).reshape(-1, 1), (EXPERTS * PAD, LANES))
    rows = jnp.concatenate([tok_slots, gate_cols, cot_slots], axis=1)
    rows = rows.reshape(EXPERTS, PAD, -1)
    rows = lax.all_to_all(rows, "ex", split_axis=0, concat_axis=0, tiled=True)
    rows = rows.reshape(EXPERTS * PAD, -1)
    kept = jnp.arange(EXPERTS * CAP)
    keep = (
        (kept // CAP * PAD + kept % CAP)[:, None] == jnp.arange(EXPERTS * PAD)[None, :]
    ).astype(BF)
    wide = features + LANES
    tok_rows = dot("kc,cd->kd", keep, rows[:, :wide]).astype(BF)
    cot_rows = dot("kc,cd->kd", keep, rows[:, wide:]).astype(BF)

    block = EXPERTS * CAP
    tok_half = lax.all_gather(tok_rows, "x", axis=0, tiled=True)
    cot_half = spread(cot_rows, ("zl", "yl"))
    cot_half, gathered = lax.optimization_barrier((cot_half, gathered))
    slot_all = spread(tok_half, ("zl", "yl"))
    slot_cotan = lax.all_gather(cot_half, "x", axis=0, tiled=True)
    slot_tokens = slot_all[:, :features]
    gathered = gathered.reshape(n_dp, 3, hidden_dev, features)

    def reorder(values):
        v = values.reshape(4, 4, block, values.shape[-1])
        return jnp.swapaxes(v, 0, 1).reshape(values.shape)

    slab = [gathered[:, j].reshape(n_dp * hidden_dev, features) for j in range(3)]
    gate_slab, up_slab, down_slab = slab
    pre_gate = reorder(dot("rd,hd->rh", slot_tokens, gate_slab))
    pre_up = reorder(dot("rd,hd->rh", slot_tokens, up_slab))
    slot_gates = reorder(slot_all[:, features : features + 1]).astype(F32)
    sigmoid_gate = jax.nn.sigmoid(pre_gate)
    activation = pre_gate * sigmoid_gate
    hidden = (activation * pre_up).astype(BF)
    back_proj = dot("rd,hd->rh", slot_cotan, down_slab)
    score = jnp.sum(hidden.astype(F32) * back_proj, axis=1, keepdims=True).astype(BF)
    scaled = slot_gates * back_proj
    d_gate = (scaled * pre_up * sigmoid_gate * (1.0 + pre_gate * (1.0 - sigmoid_gate))).astype(BF)
    d_up = (scaled * activation).astype(BF)
    hidden_gated = (slot_gates * hidden.astype(F32)).astype(BF)

    grads = jnp.stack(
        [
            dot("rd,rh->dh", slot_tokens, reorder(d_gate)).astype(BF).reshape(n_dp, -1, LANES),
            dot("rd,rh->dh", slot_tokens, reorder(d_up)).astype(BF).reshape(n_dp, -1, LANES),
            dot("rd,rh->dh", slot_cotan, hidden_gated).astype(BF).reshape(n_dp, -1, LANES),
        ],
        axis=1,
    )
    grads = lax.psum_scatter(grads, DP, scatter_dimension=0, tiled=True)[0].astype(F32)

    left = jnp.concatenate([d_gate, d_up, jnp.broadcast_to(score, d_up.shape)], axis=1)
    first = (jnp.arange(LANES) == 0).astype(BF)[:, None]
    right = jnp.concatenate(
        [
            jnp.concatenate([gate_slab, jnp.zeros((LANES, LANES), BF)], axis=1),
            jnp.concatenate([up_slab, jnp.zeros((LANES, LANES), BF)], axis=1),
            jnp.concatenate(
                [jnp.zeros((LANES, features), BF), jnp.broadcast_to(first, (LANES, LANES))], axis=1
            ),
        ],
        axis=0,
    )
    right = lax.optimization_barrier(right)
    back = dot("rh,hd->rd", left, right).astype(BF)
    back = back.reshape(8, 2 * block, wide)
    back = lax.all_to_all(back, ("x", "zl"), split_axis=0, concat_axis=0, tiled=True)
    back = back.reshape(HSPLIT * block, wide)
    row = jnp.arange(2 * block)
    target = (row // CAP % EXPERTS * 2 + row // block) * PAD + row % CAP
    fold = (jnp.arange(2 * EXPERTS * PAD)[:, None] == target[None, :]).astype(BF)
    home = dot("ck,kd->cd", jnp.tile(fold, (1, 8)), back).astype(BF)
    home = lax.all_to_all(
        home.reshape(2 * EXPERTS, PAD, wide), ("ex", "yl"), split_axis=0, concat_axis=0, tiled=True
    ).reshape(2 * EXPERTS * PAD, wide)
    pick_home = jnp.broadcast_to(pick[:, None], (EXPERTS, 2, PAD, tok_count))
    pick_home = pick_home.reshape(2 * EXPERTS * PAD, tok_count).astype(BF)
    token_grad = dot("ct,cd->td", pick_home, home[:, :features]).astype(BF)
    score_slots = jnp.sum(
        home[:, features : features + 1].astype(F32).reshape(EXPERTS, 2, PAD, 1), axis=1
    )
    score_token = jnp.sum(jnp.where(pick, score_slots, 0.0), axis=1)
    gate_grad = jnp.sum(jnp.where(hits, score_token[:, None, :], 0.0), axis=0).T

    start = lax.axis_index(DP) * (features // n_dp)
    relaid = [
        lax.dynamic_slice_in_dim(w, start, features // n_dp, axis=1).T[None] for w in slab
    ]
    return (*relaid, grads[0:1], grads[1:2], grads[2:3], token_grad, gate_grad)


def solution(mesh):
    fine = Mesh(
        mesh.devices.reshape(4, 2, 4, 2, 4, 2), ("yh", "core", "ex", "zl", "x", "yl")
    )
    expert = ("ex", "zl", "x", "yl")
    rows = P(DP + expert, None)
    weights = P(expert, None, DP)
    laid = P(expert, DP, None)
    return jax.shard_map(
        shards,
        mesh=fine,
        in_specs=(rows,) * 4 + (weights,) * 3,
        out_specs=(laid,) * 6 + (rows,) * 2,
        check_vma=False,
    )
```

```python
import jax
import jax.numpy as jnp
from jax import lax
from jax.experimental import pallas as pl
from jax.experimental.pallas import tpu as pltpu
from jax.sharding import Mesh
from jax.sharding import PartitionSpec as P

HSPLIT = 16
CAP = 6
PAD = 8
EXPERTS = 4
LANES = 128
CHUNK = 512
SPLIT = 2560
DP = ("yh", "core")
BF = jnp.bfloat16
F32 = jnp.float32


def spread(block, axes):
    count = lax.axis_size(axes)
    copies = jnp.broadcast_to(block[None], (count,) + block.shape)
    got = lax.all_to_all(copies, axes, split_axis=0, concat_axis=0, tiled=True)
    return got.reshape((count * block.shape[0],) + block.shape[1:])


def weight_grads(x, dy_low, dy_high, d_gate_up, hidden_gated, features):
    rows = x.shape[0]
    low = dy_low.shape[1] // CHUNK
    over_rows = (((0,), (0,)), ((), ()))

    def kernel(x_ref, low_ref, high_ref, d_ref, h_ref, o_ref):
        def product(a, b):
            return lax.dot_general(a, b, over_rows, preferred_element_type=F32).astype(BF)

        o_ref[:, : 2 * LANES] = product(x_ref[...], d_ref[...])

        @pl.when(pl.program_id(0) < low)
        def _():
            o_ref[:, 2 * LANES :] = product(low_ref[...], h_ref[...])

        @pl.when(pl.program_id(0) >= low)
        def _():
            o_ref[:, 2 * LANES :] = product(high_ref[...], h_ref[...])

    return pl.pallas_call(
        kernel,
        grid=(features // CHUNK,),
        in_specs=[
            pl.BlockSpec((rows, CHUNK), lambda j: (0, j)),
            pl.BlockSpec((rows, CHUNK), lambda j: (0, jnp.minimum(j, low - 1))),
            pl.BlockSpec((rows, CHUNK), lambda j: (0, jnp.maximum(j - low, 0))),
            pl.BlockSpec((rows, 2 * LANES), lambda j: (0, 0)),
            pl.BlockSpec((rows, LANES), lambda j: (0, 0)),
        ],
        out_specs=pl.BlockSpec((CHUNK, 3 * LANES), lambda j: (j, 0)),
        out_shape=jax.ShapeDtypeStruct((features, 3 * LANES), BF),
        compiler_params=pltpu.CompilerParams(vmem_limit_bytes=32 << 20),
        cost_estimate=pl.CostEstimate(
            flops=2 * rows * features * 3 * LANES,
            bytes_accessed=2 * features * (2 * rows + 3 * LANES),
            transcendentals=0,
        ),
        name="weight_grads",
    )(x, dy_low, dy_high, d_gate_up, hidden_gated)


def dot(eq, a, b):
    return jnp.einsum(eq, a, b, preferred_element_type=F32)


def shards(tokens, cotangent, route_ids, gates, w_gate, w_up, w_down):
    tok_count, features = tokens.shape
    hidden_dev = w_gate.shape[2]

    mine = jnp.concatenate([w_gate[0].T, w_up[0].T, w_down[0].T], axis=0)
    gathered = lax.all_gather(mine, DP, axis=0, tiled=True)
    n_dp = lax.axis_size(DP)

    ids = route_ids.T
    gates_t = gates.T.astype(F32)
    experts = jnp.arange(EXPERTS, dtype=jnp.int32)
    hits = ids[None] == experts[:, None, None]
    token_hit = jnp.any(hits, axis=1)
    before = (
        jnp.arange(tok_count)[:, None] < jnp.arange(tok_count)[None, :]
    ).astype(BF)
    rank = dot("et,tu->eu", token_hit.astype(BF), before)
    slots = jnp.arange(PAD, dtype=jnp.int32)
    pick = token_hit[:, None, :] & (rank.astype(jnp.int32)[:, None, :] == slots[None, :, None])
    gate_of = jnp.sum(jnp.where(hits, gates_t[None], 0.0), axis=1)
    gate_slots = jnp.sum(jnp.where(pick, gate_of[:, None, :], 0.0), axis=2)
    pick_rows = pick.reshape(EXPERTS * PAD, tok_count).astype(BF)
    tok_slots = dot("ct,td->cd", pick_rows, tokens).astype(BF)
    cot_slots = dot("ct,td->cd", pick_rows, cotangent).astype(BF)
    gate_cols = jnp.broadcast_to(gate_slots.astype(BF).reshape(-1, 1), (EXPERTS * PAD, LANES))
    rows = jnp.concatenate([tok_slots, gate_cols, cot_slots], axis=1)
    rows = rows.reshape(EXPERTS, PAD, -1)
    rows = lax.all_to_all(rows, "ex", split_axis=0, concat_axis=0, tiled=True)
    rows = rows.reshape(EXPERTS * PAD, -1)
    kept = jnp.arange(EXPERTS * CAP)
    keep = (
        (kept // CAP * PAD + kept % CAP)[:, None] == jnp.arange(EXPERTS * PAD)[None, :]
    ).astype(BF)
    wide = features + LANES
    tok_rows = dot("kc,cd->kd", keep, rows[:, :wide]).astype(BF)
    cot_rows = dot("kc,cd->kd", keep, rows[:, wide:]).astype(BF)

    block = EXPERTS * CAP
    tok_half = lax.all_gather(tok_rows, "x", axis=0, tiled=True)
    cot_half = spread(cot_rows, ("zl", "yl"))
    cot_half, gathered = lax.optimization_barrier((cot_half, gathered))
    slot_all = spread(tok_half, ("zl", "yl"))
    cot_low = lax.all_gather(cot_half[:, :SPLIT], "x", axis=0, tiled=True)
    cot_high = lax.all_gather(cot_half[:, SPLIT:], "x", axis=0, tiled=True)
    gathered = gathered.reshape(n_dp, 3, hidden_dev, features)

    def reorder(values):
        v = values.reshape(4, 4, block, values.shape[-1])
        return jnp.swapaxes(v, 0, 1).reshape(values.shape)

    slab = [gathered[:, j].reshape(n_dp * hidden_dev, features) for j in range(3)]
    gate_slab, up_slab, down_slab = slab
    pad = jnp.zeros((LANES, LANES), BF)
    wide_slab = jnp.concatenate(
        [
            jnp.concatenate([gate_slab, pad], axis=1),
            jnp.concatenate([up_slab, pad], axis=1),
            jnp.concatenate([jnp.zeros((LANES, features), BF), jnp.eye(LANES, dtype=BF)], axis=1),
        ],
        axis=0,
    )
    wide_slab = lax.optimization_barrier(wide_slab)
    both = reorder(dot("rd,hd->rh", slot_all, wide_slab))
    pre_gate = both[:, :LANES]
    pre_up = both[:, LANES : 2 * LANES]
    slot_gates = both[:, 2 * LANES :]
    sigmoid_gate = jax.nn.sigmoid(pre_gate)
    activation = pre_gate * sigmoid_gate
    hidden = (activation * pre_up).astype(BF)
    back_proj = dot("rd,hd->rh", cot_low, down_slab[:, :SPLIT]) + dot(
        "rd,hd->rh", cot_high, down_slab[:, SPLIT:]
    )
    score = jnp.sum(hidden.astype(F32) * back_proj, axis=1, keepdims=True).astype(BF)
    scaled = slot_gates * back_proj
    d_gate = (scaled * pre_up * sigmoid_gate * (1.0 + pre_gate * (1.0 - sigmoid_gate))).astype(BF)
    d_up = (scaled * activation).astype(BF)
    hidden_gated = (slot_gates * hidden.astype(F32)).astype(BF)

    left = jnp.concatenate([d_gate, d_up, jnp.broadcast_to(score, d_up.shape)], axis=1)
    back = dot("rh,hd->rd", left, wide_slab).astype(BF)
    grads = weight_grads(
        slot_all, cot_low, cot_high, reorder(left[:, : 2 * LANES]), hidden_gated, features
    )
    grads = lax.psum_scatter(grads, DP, scatter_dimension=0, tiled=True).astype(F32)
    grads = [grads[None, :, LANES * j : LANES * (j + 1)] for j in range(3)]

    back = back.reshape(8, 2 * block, wide)
    back = lax.all_to_all(back, ("x", "zl"), split_axis=0, concat_axis=0, tiled=True)
    back = back.reshape(HSPLIT * block, wide)
    row = jnp.arange(2 * block)
    target = (row // CAP % EXPERTS * 2 + row // block) * PAD + row % CAP
    fold = (jnp.arange(2 * EXPERTS * PAD)[:, None] == target[None, :]).astype(BF)
    home = dot("ck,kd->cd", jnp.tile(fold, (1, 8)), back).astype(BF)
    home = lax.all_to_all(
        home.reshape(2 * EXPERTS, PAD, wide), ("ex", "yl"), split_axis=0, concat_axis=0, tiled=True
    ).reshape(2 * EXPERTS * PAD, wide)
    pick_home = jnp.broadcast_to(pick[:, None], (EXPERTS, 2, PAD, tok_count))
    pick_home = pick_home.reshape(2 * EXPERTS * PAD, tok_count).astype(BF)
    token_grad = dot("ct,cd->td", pick_home, home[:, :features]).astype(BF)
    score_slots = jnp.sum(
        home[:, features : features + 1].astype(F32).reshape(EXPERTS, 2, PAD, 1), axis=1
    )
    score_token = jnp.sum(jnp.where(pick, score_slots, 0.0), axis=1)
    gate_grad = jnp.sum(jnp.where(hits, score_token[:, None, :], 0.0), axis=0).T

    start = lax.axis_index(DP) * (features // n_dp)
    relaid = [
        lax.dynamic_slice_in_dim(w, start, features // n_dp, axis=1).T[None] for w in slab
    ]
    return (*relaid, *grads, token_grad, gate_grad)


def solution(mesh):
    fine = Mesh(
        mesh.devices.reshape(4, 2, 4, 2, 4, 2), ("yh", "core", "ex", "zl", "x", "yl")
    )
    expert = ("ex", "zl", "x", "yl")
    rows = P(DP + expert, None)
    weights = P(expert, None, DP)
    laid = P(expert, DP, None)
    return jax.shard_map(
        shards,
        mesh=fine,
        in_specs=(rows,) * 4 + (weights,) * 3,
        out_specs=(laid,) * 6 + (rows,) * 2,
        check_vma=False,
    )
```

```python
import jax
import jax.numpy as jnp
from jax import lax
from jax.experimental import pallas as pl
from jax.experimental.pallas import tpu as pltpu
from jax.sharding import Mesh
from jax.sharding import PartitionSpec as P

HSPLIT = 16
CAP = 6
PAD = 8
EXPERTS = 4
LANES = 128
CHUNK = 512
SPLIT = 2560
DP = ("yh", "core")
BF = jnp.bfloat16
F32 = jnp.float32


def spread(block, axes):
    count = lax.axis_size(axes)
    copies = jnp.broadcast_to(block[None], (count,) + block.shape)
    got = lax.all_to_all(copies, axes, split_axis=0, concat_axis=0, tiled=True)
    return got.reshape((count * block.shape[0],) + block.shape[1:])


def slab_math(x, dy_low, dy_high, weights, features):
    rows, wide = x.shape
    block = rows // HSPLIT
    steps = features // CHUNK
    low = dy_low.shape[1] // CHUNK
    n_dp, _, hidden_dev, _ = weights.shape
    by_columns = (((1,), (1,)), ((), ()))
    by_rows = (((0,), (0,)), ((), ()))

    def column(j):
        return jnp.where(j < steps, j, jnp.minimum(j - steps, steps - 1))

    def kernel(
        x_ref, gate_ref, low_ref, high_ref, w_ref, back_ref, grad_ref, au, q, d_tok, d_cot, hg, score, d_tok_h, d_cot_h, hg_h
    ):
        j = pl.program_id(0)
        at = column(j)

        def slab(which):
            return w_ref[:, which].reshape(n_dp * hidden_dev, CHUNK)

        @pl.when(j == 0)
        def _():
            au[...] = jnp.zeros_like(au)
            q[...] = jnp.zeros_like(q)

        @pl.when(j < steps)
        def _():
            both = jnp.concatenate([slab(0), slab(1)], axis=0)
            au[...] += lax.dot_general(x_ref[...], both, by_columns, preferred_element_type=F32)

        @pl.when((j < steps) & (at < low))
        def _():
            q[...] += lax.dot_general(low_ref[...], slab(2), by_columns, preferred_element_type=F32)

        @pl.when((j < steps) & (at >= low))
        def _():
            q[...] += lax.dot_general(high_ref[...], slab(2), by_columns, preferred_element_type=F32)

        @pl.when(j == steps - 1)
        def _():
            for i in range(HSPLIT):
                tok = slice(i * block, (i + 1) * block)
                first = (i % 4 * 4 + i // 4) * block
                cot = slice(first, first + block)
                a = au[tok, :LANES]
                u = au[tok, LANES:]
                gate = gate_ref[tok, :].astype(F32)
                back_proj = q[cot, :]
                sigmoid = jax.nn.sigmoid(a)
                act = a * sigmoid
                hidden = (act * u).astype(BF).astype(F32)
                scaled = gate * back_proj
                d_gate = scaled * u * sigmoid * (1.0 + a * (1.0 - sigmoid))
                d_up = scaled * act
                d_tok[tok, :LANES] = d_gate
                d_tok[tok, LANES:] = d_up
                d_cot[cot, :LANES] = d_gate
                d_cot[cot, LANES:] = d_up
                hg[cot, :] = gate * hidden
                part = jnp.sum(hidden * back_proj, axis=1, keepdims=True)
                score[cot, :] = jnp.broadcast_to(part, (block, LANES))
            d_tok_h[...] = d_tok[...].astype(BF)
            d_cot_h[...] = d_cot[...].astype(BF)
            hg_h[...] = hg[...].astype(BF)

        @pl.when((j >= steps) & (j < 2 * steps))
        def _():
            both = jnp.concatenate([slab(0), slab(1)], axis=0)
            back_ref[...] = jnp.dot(d_cot_h[...], both, preferred_element_type=F32).astype(BF)
            grad_ref[:, : 2 * LANES] = lax.dot_general(
                x_ref[...], d_tok_h[...], by_rows, preferred_element_type=F32
            ).astype(BF)

        @pl.when((j >= steps) & (j < 2 * steps) & (at < low))
        def _():
            grad_ref[:, 2 * LANES :] = lax.dot_general(
                low_ref[...], hg_h[...], by_rows, preferred_element_type=F32
            ).astype(BF)

        @pl.when((j >= steps) & (j < 2 * steps) & (at >= low))
        def _():
            grad_ref[:, 2 * LANES :] = lax.dot_general(
                high_ref[...], hg_h[...], by_rows, preferred_element_type=F32
            ).astype(BF)

        @pl.when(j == 2 * steps)
        def _():
            back_ref[:, :LANES] = score[...].astype(BF)

    return pl.pallas_call(
        kernel,
        grid=(2 * steps + 1,),
        in_specs=[
            pl.BlockSpec((rows, CHUNK), lambda j: (0, column(j))),
            pl.BlockSpec((rows, LANES), lambda j: (0, features // LANES)),
            pl.BlockSpec((rows, CHUNK), lambda j: (0, jnp.minimum(column(j), low - 1))),
            pl.BlockSpec((rows, CHUNK), lambda j: (0, jnp.maximum(column(j) - low, 0))),
            pl.BlockSpec((n_dp, 3, hidden_dev, CHUNK), lambda j: (0, 0, 0, column(j))),
        ],
        out_specs=[
            pl.BlockSpec((rows, CHUNK), lambda j: (0, jnp.maximum(j - steps, 0))),
            pl.BlockSpec(
                (CHUNK, 3 * LANES), lambda j: (jnp.clip(j - steps, 0, steps - 1), 0)
            ),
        ],
        out_shape=[
            jax.ShapeDtypeStruct((rows, wide), BF),
            jax.ShapeDtypeStruct((features, 3 * LANES), BF),
        ],
        scratch_shapes=[
            pltpu.VMEM((rows, 2 * LANES), F32),
            pltpu.VMEM((rows, LANES), F32),
            pltpu.VMEM((rows, 2 * LANES), F32),
            pltpu.VMEM((rows, 2 * LANES), F32),
            pltpu.VMEM((rows, LANES), F32),
            pltpu.VMEM((rows, LANES), F32),
            pltpu.VMEM((rows, 2 * LANES), BF),
            pltpu.VMEM((rows, 2 * LANES), BF),
            pltpu.VMEM((rows, LANES), BF),
        ],
        compiler_params=pltpu.CompilerParams(vmem_limit_bytes=56 << 20),
        cost_estimate=pl.CostEstimate(
            flops=2 * rows * features * 8 * LANES,
            bytes_accessed=2 * features * (6 * rows + 9 * LANES),
            transcendentals=rows * LANES,
        ),
        name="slab_math",
    )(x, x, dy_low, dy_high, weights)


def dot(eq, a, b):
    return jnp.einsum(eq, a, b, preferred_element_type=F32)


def shards(tokens, cotangent, route_ids, gates, w_gate, w_up, w_down):
    tok_count, features = tokens.shape
    hidden_dev = w_gate.shape[2]

    mine = jnp.concatenate([w_gate[0].T, w_up[0].T, w_down[0].T], axis=0)
    gathered = lax.all_gather(mine, DP, axis=0, tiled=True)
    n_dp = lax.axis_size(DP)

    ids = route_ids.T
    gates_t = gates.T.astype(F32)
    experts = jnp.arange(EXPERTS, dtype=jnp.int32)
    hits = ids[None] == experts[:, None, None]
    token_hit = jnp.any(hits, axis=1)
    before = (
        jnp.arange(tok_count)[:, None] < jnp.arange(tok_count)[None, :]
    ).astype(BF)
    rank = dot("et,tu->eu", token_hit.astype(BF), before)
    slots = jnp.arange(PAD, dtype=jnp.int32)
    pick = token_hit[:, None, :] & (rank.astype(jnp.int32)[:, None, :] == slots[None, :, None])
    gate_of = jnp.sum(jnp.where(hits, gates_t[None], 0.0), axis=1)
    gate_slots = jnp.sum(jnp.where(pick, gate_of[:, None, :], 0.0), axis=2)
    pick_rows = pick.reshape(EXPERTS * PAD, tok_count).astype(BF)
    tok_slots = dot("ct,td->cd", pick_rows, tokens).astype(BF)
    cot_slots = dot("ct,td->cd", pick_rows, cotangent).astype(BF)
    gate_cols = jnp.broadcast_to(gate_slots.astype(BF).reshape(-1, 1), (EXPERTS * PAD, LANES))
    rows = jnp.concatenate([tok_slots, gate_cols, cot_slots], axis=1)
    rows = rows.reshape(EXPERTS, PAD, -1)
    rows = lax.all_to_all(rows, "ex", split_axis=0, concat_axis=0, tiled=True)
    rows = rows.reshape(EXPERTS * PAD, -1)
    kept = jnp.arange(EXPERTS * CAP)
    keep = (
        (kept // CAP * PAD + kept % CAP)[:, None] == jnp.arange(EXPERTS * PAD)[None, :]
    ).astype(BF)
    wide = features + LANES
    tok_rows = dot("kc,cd->kd", keep, rows[:, :wide]).astype(BF)
    cot_rows = dot("kc,cd->kd", keep, rows[:, wide:]).astype(BF)

    block = EXPERTS * CAP
    tok_half = lax.all_gather(tok_rows, "x", axis=0, tiled=True)
    cot_half = spread(cot_rows, ("zl", "yl"))
    cot_half, gathered = lax.optimization_barrier((cot_half, gathered))
    slot_all = spread(tok_half, ("zl", "yl"))
    cot_low = lax.all_gather(cot_half[:, :SPLIT], "x", axis=0, tiled=True)
    cot_high = lax.all_gather(cot_half[:, SPLIT:], "x", axis=0, tiled=True)
    gathered = gathered.reshape(n_dp, 3, hidden_dev, features)

    slab = [gathered[:, j].reshape(n_dp * hidden_dev, features) for j in range(3)]
    back, grads = slab_math(slot_all, cot_low, cot_high, gathered, features)
    grads = lax.psum_scatter(grads, DP, scatter_dimension=0, tiled=True).astype(F32)
    grads = [grads[None, :, LANES * j : LANES * (j + 1)] for j in range(3)]

    back = back.reshape(8, 2 * block, wide)
    back = lax.all_to_all(back, ("x", "zl"), split_axis=0, concat_axis=0, tiled=True)
    back = back.reshape(HSPLIT * block, wide)
    row = jnp.arange(2 * block)
    target = (row // CAP % EXPERTS * 2 + row // block) * PAD + row % CAP
    fold = (jnp.arange(2 * EXPERTS * PAD)[:, None] == target[None, :]).astype(BF)
    home = dot("ck,kd->cd", jnp.tile(fold, (1, 8)), back).astype(BF)
    home = lax.all_to_all(
        home.reshape(2 * EXPERTS, PAD, wide), ("ex", "yl"), split_axis=0, concat_axis=0, tiled=True
    ).reshape(2 * EXPERTS * PAD, wide)
    pick_home = jnp.broadcast_to(pick[:, None], (EXPERTS, 2, PAD, tok_count))
    pick_home = pick_home.reshape(2 * EXPERTS * PAD, tok_count).astype(BF)
    token_grad = dot("ct,cd->td", pick_home, home[:, :features]).astype(BF)
    score_slots = jnp.sum(
        home[:, features : features + 1].astype(F32).reshape(EXPERTS, 2, PAD, 1), axis=1
    )
    score_token = jnp.sum(jnp.where(pick, score_slots, 0.0), axis=1)
    gate_grad = jnp.sum(jnp.where(hits, score_token[:, None, :], 0.0), axis=0).T

    start = lax.axis_index(DP) * (features // n_dp)
    relaid = [
        lax.dynamic_slice_in_dim(w, start, features // n_dp, axis=1).T[None] for w in slab
    ]
    return (*relaid, *grads, token_grad, gate_grad)


def solution(mesh):
    fine = Mesh(
        mesh.devices.reshape(4, 2, 4, 2, 4, 2), ("yh", "core", "ex", "zl", "x", "yl")
    )
    expert = ("ex", "zl", "x", "yl")
    rows = P(DP + expert, None)
    weights = P(expert, None, DP)
    laid = P(expert, DP, None)
    return jax.shard_map(
        shards,
        mesh=fine,
        in_specs=(rows,) * 4 + (weights,) * 3,
        out_specs=(laid,) * 6 + (rows,) * 2,
        check_vma=False,
    )
```

```python
import jax
import jax.numpy as jnp
from jax import lax
from jax.experimental import pallas as pl
from jax.experimental.pallas import tpu as pltpu
from jax.sharding import Mesh
from jax.sharding import PartitionSpec as P

HSPLIT = 16
CAP = 6
PAD = 8
EXPERTS = 4
LANES = 128
CHUNK = 512
SPLIT = 2560
DP = ("yh", "core")
BF = jnp.bfloat16
F32 = jnp.float32


def spread(block, axes):
    count = lax.axis_size(axes)
    copies = jnp.broadcast_to(block[None], (count,) + block.shape)
    got = lax.all_to_all(copies, axes, split_axis=0, concat_axis=0, tiled=True)
    return got.reshape((count * block.shape[0],) + block.shape[1:])


def weight_grads(x, dy_low, dy_high, d_gate_up, hidden_gated, features):
    rows = x.shape[0]
    low = dy_low.shape[1] // CHUNK

    def kernel(x_ref, low_ref, high_ref, d_ref, h_ref, o_ref, d_turned, h_turned):
        def product(turned, columns):
            out = jnp.dot(turned[...], columns[...], preferred_element_type=F32)
            return out.astype(BF).T

        @pl.when(pl.program_id(0) == 0)
        def _():
            d_turned[...] = d_ref[...].T
            h_turned[...] = h_ref[...].T

        o_ref[:, : 2 * LANES] = product(d_turned, x_ref)

        @pl.when(pl.program_id(0) < low)
        def _():
            o_ref[:, 2 * LANES :] = product(h_turned, low_ref)

        @pl.when(pl.program_id(0) >= low)
        def _():
            o_ref[:, 2 * LANES :] = product(h_turned, high_ref)

    return pl.pallas_call(
        kernel,
        grid=(features // CHUNK,),
        in_specs=[
            pl.BlockSpec((rows, CHUNK), lambda j: (0, j)),
            pl.BlockSpec((rows, CHUNK), lambda j: (0, jnp.minimum(j, low - 1))),
            pl.BlockSpec((rows, CHUNK), lambda j: (0, jnp.maximum(j - low, 0))),
            pl.BlockSpec((rows, 2 * LANES), lambda j: (0, 0)),
            pl.BlockSpec((rows, LANES), lambda j: (0, 0)),
        ],
        out_specs=pl.BlockSpec((CHUNK, 3 * LANES), lambda j: (j, 0)),
        out_shape=jax.ShapeDtypeStruct((features, 3 * LANES), BF),
        scratch_shapes=[pltpu.VMEM((2 * LANES, rows), BF), pltpu.VMEM((LANES, rows), BF)],
        compiler_params=pltpu.CompilerParams(vmem_limit_bytes=58 << 20),
        cost_estimate=pl.CostEstimate(
            flops=2 * rows * features * 3 * LANES,
            bytes_accessed=2 * features * (2 * rows + 3 * LANES),
            transcendentals=0,
        ),
        name="weight_grads",
    )(x, dy_low, dy_high, d_gate_up, hidden_gated)


def dot(eq, a, b):
    return jnp.einsum(eq, a, b, preferred_element_type=F32)


def shards(tokens, cotangent, route_ids, gates, w_gate, w_up, w_down):
    tok_count, features = tokens.shape
    hidden_dev = w_gate.shape[2]

    mine = jnp.concatenate([w_gate[0].T, w_up[0].T, w_down[0].T], axis=0)
    gathered = lax.all_gather(mine, DP, axis=0, tiled=True)
    n_dp = lax.axis_size(DP)

    ids = route_ids.T
    gates_t = gates.T.astype(F32)
    experts = jnp.arange(EXPERTS, dtype=jnp.int32)
    hits = ids[None] == experts[:, None, None]
    token_hit = jnp.any(hits, axis=1)
    before = (
        jnp.arange(tok_count)[:, None] < jnp.arange(tok_count)[None, :]
    ).astype(BF)
    rank = dot("et,tu->eu", token_hit.astype(BF), before)
    slots = jnp.arange(PAD, dtype=jnp.int32)
    pick = token_hit[:, None, :] & (rank.astype(jnp.int32)[:, None, :] == slots[None, :, None])
    gate_of = jnp.sum(jnp.where(hits, gates_t[None], 0.0), axis=1)
    gate_slots = jnp.sum(jnp.where(pick, gate_of[:, None, :], 0.0), axis=2)
    pick_rows = pick.reshape(EXPERTS * PAD, tok_count).astype(BF)
    tok_slots = dot("ct,td->cd", pick_rows, tokens).astype(BF)
    cot_slots = dot("ct,td->cd", pick_rows, cotangent).astype(BF)
    gate_cols = jnp.broadcast_to(gate_slots.astype(BF).reshape(-1, 1), (EXPERTS * PAD, LANES))
    rows = jnp.concatenate([tok_slots, gate_cols, cot_slots], axis=1)
    rows = rows.reshape(EXPERTS, PAD, -1)
    rows = lax.all_to_all(rows, "ex", split_axis=0, concat_axis=0, tiled=True)
    rows = rows.reshape(EXPERTS * PAD, -1)
    kept = jnp.arange(EXPERTS * CAP)
    keep = (
        (kept // CAP * PAD + kept % CAP)[:, None] == jnp.arange(EXPERTS * PAD)[None, :]
    ).astype(BF)
    wide = features + LANES
    tok_rows = dot("kc,cd->kd", keep, rows[:, :wide]).astype(BF)
    cot_rows = dot("kc,cd->kd", keep, rows[:, wide:]).astype(BF)

    block = EXPERTS * CAP
    tok_half = lax.all_gather(tok_rows, "x", axis=0, tiled=True)
    cot_half = spread(cot_rows, ("zl", "yl"))
    cot_half, gathered = lax.optimization_barrier((cot_half, gathered))
    slot_all = spread(tok_half, ("zl", "yl"))
    cot_low = lax.all_gather(cot_half[:, :SPLIT], "x", axis=0, tiled=True)
    cot_high = lax.all_gather(cot_half[:, SPLIT:], "x", axis=0, tiled=True)
    gathered = gathered.reshape(n_dp, 3, hidden_dev, features)

    def reorder(values):
        v = values.reshape(4, 4, block, values.shape[-1])
        return jnp.swapaxes(v, 0, 1).reshape(values.shape)

    slab = [gathered[:, j].reshape(n_dp * hidden_dev, features) for j in range(3)]
    gate_slab, up_slab, down_slab = slab
    pad = jnp.zeros((LANES, LANES), BF)
    wide_slab = jnp.concatenate(
        [
            jnp.concatenate([gate_slab, pad], axis=1),
            jnp.concatenate([up_slab, pad], axis=1),
            jnp.concatenate([jnp.zeros((LANES, features), BF), jnp.eye(LANES, dtype=BF)], axis=1),
        ],
        axis=0,
    )
    wide_slab = lax.optimization_barrier(wide_slab)
    both = reorder(dot("rd,hd->rh", slot_all, wide_slab))
    pre_gate = both[:, :LANES]
    pre_up = both[:, LANES : 2 * LANES]
    slot_gates = both[:, 2 * LANES :]
    sigmoid_gate = jax.nn.sigmoid(pre_gate)
    activation = pre_gate * sigmoid_gate
    hidden = (activation * pre_up).astype(BF)
    back_proj = dot("rd,hd->rh", cot_low, down_slab[:, :SPLIT]) + dot(
        "rd,hd->rh", cot_high, down_slab[:, SPLIT:]
    )
    score = jnp.sum(hidden.astype(F32) * back_proj, axis=1, keepdims=True).astype(BF)
    scaled = slot_gates * back_proj
    d_gate = (scaled * pre_up * sigmoid_gate * (1.0 + pre_gate * (1.0 - sigmoid_gate))).astype(BF)
    d_up = (scaled * activation).astype(BF)
    hidden_gated = (slot_gates * hidden.astype(F32)).astype(BF)

    left = jnp.concatenate([d_gate, d_up, jnp.broadcast_to(score, d_up.shape)], axis=1)
    back = dot("rh,hd->rd", left, wide_slab).astype(BF)
    grads = weight_grads(
        slot_all, cot_low, cot_high, reorder(left[:, : 2 * LANES]), hidden_gated, features
    )
    grads = lax.psum_scatter(grads, DP, scatter_dimension=0, tiled=True).astype(F32)
    grads = [grads[None, :, LANES * j : LANES * (j + 1)] for j in range(3)]

    back = back.reshape(8, 2 * block, wide)
    back = lax.all_to_all(back, ("x", "zl"), split_axis=0, concat_axis=0, tiled=True)
    back = back.reshape(HSPLIT * block, wide)
    row = jnp.arange(2 * block)
    target = (row // CAP % EXPERTS * 2 + row // block) * PAD + row % CAP
    fold = (jnp.arange(2 * EXPERTS * PAD)[:, None] == target[None, :]).astype(BF)
    home = dot("ck,kd->cd", jnp.tile(fold, (1, 8)), back).astype(BF)
    home = lax.all_to_all(
        home.reshape(2 * EXPERTS, PAD, wide), ("ex", "yl"), split_axis=0, concat_axis=0, tiled=True
    ).reshape(2 * EXPERTS * PAD, wide)
    pick_home = jnp.broadcast_to(pick[:, None], (EXPERTS, 2, PAD, tok_count))
    pick_home = pick_home.reshape(2 * EXPERTS * PAD, tok_count).astype(BF)
    token_grad = dot("ct,cd->td", pick_home, home[:, :features]).astype(BF)
    score_slots = jnp.sum(
        home[:, features : features + 1].astype(F32).reshape(EXPERTS, 2, PAD, 1), axis=1
    )
    score_token = jnp.sum(jnp.where(pick, score_slots, 0.0), axis=1)
    gate_grad = jnp.sum(jnp.where(hits, score_token[:, None, :], 0.0), axis=0).T

    start = lax.axis_index(DP) * (features // n_dp)
    relaid = [
        lax.dynamic_slice_in_dim(w, start, features // n_dp, axis=1).T[None] for w in slab
    ]
    return (*relaid, *grads, token_grad, gate_grad)


def solution(mesh):
    fine = Mesh(
        mesh.devices.reshape(4, 2, 4, 2, 4, 2), ("yh", "core", "ex", "zl", "x", "yl")
    )
    expert = ("ex", "zl", "x", "yl")
    rows = P(DP + expert, None)
    weights = P(expert, None, DP)
    laid = P(expert, DP, None)
    return jax.shard_map(
        shards,
        mesh=fine,
        in_specs=(rows,) * 4 + (weights,) * 3,
        out_specs=(laid,) * 6 + (rows,) * 2,
        check_vma=False,
    )
```

```python
import jax
import jax.numpy as jnp
from jax import lax
from jax.experimental import pallas as pl
from jax.experimental.pallas import tpu as pltpu
from jax.sharding import Mesh
from jax.sharding import PartitionSpec as P

HSPLIT = 16
CAP = 6
PAD = 8
EXPERTS = 4
LANES = 128
CHUNK = 512
SPLIT = 2560
DP = ("yh", "core")
BF = jnp.bfloat16
F32 = jnp.float32


def spread(block, axes):
    count = lax.axis_size(axes)
    copies = jnp.broadcast_to(block[None], (count,) + block.shape)
    got = lax.all_to_all(copies, axes, split_axis=0, concat_axis=0, tiled=True)
    return got.reshape((count * block.shape[0],) + block.shape[1:])


def weight_grads(x, dy_low, dy_high, d_gate_up, hidden_gated, features):
    rows = x.shape[0]
    low = dy_low.shape[1] // CHUNK
    over_rows = (((0,), (0,)), ((), ()))

    def kernel(x_ref, low_ref, high_ref, d_ref, h_ref, o_ref):
        def product(a, b):
            return lax.dot_general(a, b, over_rows, preferred_element_type=F32).astype(BF)

        o_ref[:, : 2 * LANES] = product(x_ref[...], d_ref[...])

        @pl.when(pl.program_id(0) < low)
        def _():
            o_ref[:, 2 * LANES :] = product(low_ref[...], h_ref[...])

        @pl.when(pl.program_id(0) >= low)
        def _():
            o_ref[:, 2 * LANES :] = product(high_ref[...], h_ref[...])

    return pl.pallas_call(
        kernel,
        grid=(features // CHUNK,),
        in_specs=[
            pl.BlockSpec((rows, CHUNK), lambda j: (0, j)),
            pl.BlockSpec((rows, CHUNK), lambda j: (0, jnp.minimum(j, low - 1))),
            pl.BlockSpec((rows, CHUNK), lambda j: (0, jnp.maximum(j - low, 0))),
            pl.BlockSpec((rows, 2 * LANES), lambda j: (0, 0)),
            pl.BlockSpec((rows, LANES), lambda j: (0, 0)),
        ],
        out_specs=pl.BlockSpec((CHUNK, 3 * LANES), lambda j: (j, 0)),
        out_shape=jax.ShapeDtypeStruct((features, 3 * LANES), BF),
        compiler_params=pltpu.CompilerParams(vmem_limit_bytes=32 << 20),
        cost_estimate=pl.CostEstimate(
            flops=2 * rows * features * 3 * LANES,
            bytes_accessed=2 * features * (2 * rows + 3 * LANES),
            transcendentals=0,
        ),
        name="weight_grads",
    )(x, dy_low, dy_high, d_gate_up, hidden_gated)


def dot(eq, a, b):
    return jnp.einsum(eq, a, b, preferred_element_type=F32)


def shards(tokens, cotangent, route_ids, gates, w_gate, w_up, w_down):
    tok_count, features = tokens.shape
    hidden_dev = w_gate.shape[2]

    mine = jnp.concatenate([w_gate[0].T, w_up[0].T, w_down[0].T], axis=0)
    gathered = lax.all_gather(mine, "yh", axis=0, tiled=True)
    n_dp = lax.axis_size(DP)

    ids = route_ids.T
    gates_t = gates.T.astype(F32)
    experts = jnp.arange(EXPERTS, dtype=jnp.int32)
    hits = ids[None] == experts[:, None, None]
    token_hit = jnp.any(hits, axis=1)
    before = (
        jnp.arange(tok_count)[:, None] < jnp.arange(tok_count)[None, :]
    ).astype(BF)
    rank = dot("et,tu->eu", token_hit.astype(BF), before)
    slots = jnp.arange(PAD, dtype=jnp.int32)
    pick = token_hit[:, None, :] & (rank.astype(jnp.int32)[:, None, :] == slots[None, :, None])
    gate_of = jnp.sum(jnp.where(hits, gates_t[None], 0.0), axis=1)
    gate_slots = jnp.sum(jnp.where(pick, gate_of[:, None, :], 0.0), axis=2)
    pick_rows = pick.reshape(EXPERTS * PAD, tok_count).astype(BF)
    tok_slots = dot("ct,td->cd", pick_rows, tokens).astype(BF)
    cot_slots = dot("ct,td->cd", pick_rows, cotangent).astype(BF)
    gate_cols = jnp.broadcast_to(gate_slots.astype(BF).reshape(-1, 1), (EXPERTS * PAD, LANES))
    rows = jnp.concatenate([tok_slots, gate_cols, cot_slots], axis=1)
    rows = rows.reshape(EXPERTS, PAD, -1)
    rows = lax.all_to_all(rows, "ex", split_axis=0, concat_axis=0, tiled=True)
    rows = rows.reshape(EXPERTS * PAD, -1)
    kept = jnp.arange(EXPERTS * CAP)
    keep = (
        (kept // CAP * PAD + kept % CAP)[:, None] == jnp.arange(EXPERTS * PAD)[None, :]
    ).astype(BF)
    wide = features + LANES
    tok_rows = dot("kc,cd->kd", keep, rows[:, :wide]).astype(BF)
    cot_rows = dot("kc,cd->kd", keep, rows[:, wide:]).astype(BF)

    block = EXPERTS * CAP
    tok_half = lax.all_gather(tok_rows, "x", axis=0, tiled=True)
    cot_half = spread(cot_rows, ("zl", "yl"))
    tok_half, cot_half, gathered = lax.optimization_barrier((tok_half, cot_half, gathered))
    slot_all = spread(tok_half, ("zl", "yl"))
    cot_low = lax.all_gather(cot_half[:, :SPLIT], "x", axis=0, tiled=True)
    cot_high = lax.all_gather(cot_half[:, SPLIT:], "x", axis=0, tiled=True)
    other = lax.ppermute(gathered, "core", [(0, 1), (1, 0)])
    even = lax.axis_index("core") == 0
    gathered = jnp.stack(
        [
            jnp.where(even, mixed[0], mixed[1]).reshape(n_dp // 2, 3, hidden_dev, features)
            for mixed in ((gathered, other), (other, gathered))
        ],
        axis=1,
    ).reshape(n_dp, 3, hidden_dev, features)

    def reorder(values):
        v = values.reshape(4, 4, block, values.shape[-1])
        return jnp.swapaxes(v, 0, 1).reshape(values.shape)

    slab = [gathered[:, j].reshape(n_dp * hidden_dev, features) for j in range(3)]
    gate_slab, up_slab, down_slab = slab
    pad = jnp.zeros((LANES, LANES), BF)
    wide_slab = jnp.concatenate(
        [
            jnp.concatenate([gate_slab, pad], axis=1),
            jnp.concatenate([up_slab, pad], axis=1),
            jnp.concatenate([jnp.zeros((LANES, features), BF), jnp.eye(LANES, dtype=BF)], axis=1),
        ],
        axis=0,
    )
    wide_slab = lax.optimization_barrier(wide_slab)
    both = reorder(dot("rd,hd->rh", slot_all, wide_slab))
    pre_gate = both[:, :LANES]
    pre_up = both[:, LANES : 2 * LANES]
    slot_gates = both[:, 2 * LANES :]
    sigmoid_gate = jax.nn.sigmoid(pre_gate)
    activation = pre_gate * sigmoid_gate
    hidden = (activation * pre_up).astype(BF)
    back_proj = dot("rd,hd->rh", cot_low, down_slab[:, :SPLIT]) + dot(
        "rd,hd->rh", cot_high, down_slab[:, SPLIT:]
    )
    score = jnp.sum(hidden.astype(F32) * back_proj, axis=1, keepdims=True).astype(BF)
    scaled = slot_gates * back_proj
    d_gate = (scaled * pre_up * sigmoid_gate * (1.0 + pre_gate * (1.0 - sigmoid_gate))).astype(BF)
    d_up = (scaled * activation).astype(BF)
    hidden_gated = (slot_gates * hidden.astype(F32)).astype(BF)

    left = jnp.concatenate([d_gate, d_up, jnp.broadcast_to(score, d_up.shape)], axis=1)
    back = dot("rh,hd->rd", left, wide_slab).astype(BF)
    grads = weight_grads(
        slot_all, cot_low, cot_high, reorder(left[:, : 2 * LANES]), hidden_gated, features
    )
    grads = lax.psum_scatter(grads, DP, scatter_dimension=0, tiled=True).astype(F32)
    grads = [grads[None, :, LANES * j : LANES * (j + 1)] for j in range(3)]

    back = back.reshape(8, 2 * block, wide)
    back = lax.all_to_all(back, ("x", "zl"), split_axis=0, concat_axis=0, tiled=True)
    back = back.reshape(HSPLIT * block, wide)
    row = jnp.arange(2 * block)
    target = (row // CAP % EXPERTS * 2 + row // block) * PAD + row % CAP
    fold = (jnp.arange(2 * EXPERTS * PAD)[:, None] == target[None, :]).astype(BF)
    home = dot("ck,kd->cd", jnp.tile(fold, (1, 8)), back).astype(BF)
    home = lax.all_to_all(
        home.reshape(2 * EXPERTS, PAD, wide), ("ex", "yl"), split_axis=0, concat_axis=0, tiled=True
    ).reshape(2 * EXPERTS * PAD, wide)
    pick_home = jnp.broadcast_to(pick[:, None], (EXPERTS, 2, PAD, tok_count))
    pick_home = pick_home.reshape(2 * EXPERTS * PAD, tok_count).astype(BF)
    token_grad = dot("ct,cd->td", pick_home, home[:, :features]).astype(BF)
    score_slots = jnp.sum(
        home[:, features : features + 1].astype(F32).reshape(EXPERTS, 2, PAD, 1), axis=1
    )
    score_token = jnp.sum(jnp.where(pick, score_slots, 0.0), axis=1)
    gate_grad = jnp.sum(jnp.where(hits, score_token[:, None, :], 0.0), axis=0).T

    start = lax.axis_index(DP) * (features // n_dp)
    relaid = [
        lax.dynamic_slice_in_dim(w, start, features // n_dp, axis=1).T[None] for w in slab
    ]
    return (*relaid, *grads, token_grad, gate_grad)


def solution(mesh):
    fine = Mesh(
        mesh.devices.reshape(4, 2, 4, 2, 4, 2), ("yh", "core", "ex", "zl", "x", "yl")
    )
    expert = ("ex", "zl", "x", "yl")
    rows = P(DP + expert, None)
    weights = P(expert, None, DP)
    laid = P(expert, DP, None)
    return jax.shard_map(
        shards,
        mesh=fine,
        in_specs=(rows,) * 4 + (weights,) * 3,
        out_specs=(laid,) * 6 + (rows,) * 2,
        check_vma=False,
    )
```

```python
import jax
import jax.numpy as jnp
from jax import lax
from jax.experimental import pallas as pl
from jax.experimental.pallas import tpu as pltpu
from jax.sharding import Mesh
from jax.sharding import PartitionSpec as P

HSPLIT = 16
CAP = 6
PAD = 8
EXPERTS = 4
LANES = 128
CHUNK = 512
SPLIT = 2560
DP = ("yh", "core")
BF = jnp.bfloat16
F32 = jnp.float32


def spread(block, axes):
    count = lax.axis_size(axes)
    copies = jnp.broadcast_to(block[None], (count,) + block.shape)
    got = lax.all_to_all(copies, axes, split_axis=0, concat_axis=0, tiled=True)
    return got.reshape((count * block.shape[0],) + block.shape[1:])


def weight_grads(x, dy_low, dy_high, d_gate_up, hidden_gated, features):
    rows = x.shape[0]
    low = dy_low.shape[1] // CHUNK
    over_rows = (((0,), (0,)), ((), ()))

    def kernel(x_ref, low_ref, high_ref, d_ref, h_ref, o_ref):
        def product(a, b):
            return lax.dot_general(a, b, over_rows, preferred_element_type=F32).astype(BF)

        o_ref[:, : 2 * LANES] = product(x_ref[...], d_ref[...])

        @pl.when(pl.program_id(0) < low)
        def _():
            o_ref[:, 2 * LANES :] = product(low_ref[...], h_ref[...])

        @pl.when(pl.program_id(0) >= low)
        def _():
            o_ref[:, 2 * LANES :] = product(high_ref[...], h_ref[...])

    return pl.pallas_call(
        kernel,
        grid=(features // CHUNK,),
        in_specs=[
            pl.BlockSpec((rows, CHUNK), lambda j: (0, j)),
            pl.BlockSpec((rows, CHUNK), lambda j: (0, jnp.minimum(j, low - 1))),
            pl.BlockSpec((rows, CHUNK), lambda j: (0, jnp.maximum(j - low, 0))),
            pl.BlockSpec((rows, 2 * LANES), lambda j: (0, 0)),
            pl.BlockSpec((rows, LANES), lambda j: (0, 0)),
        ],
        out_specs=pl.BlockSpec((CHUNK, 3 * LANES), lambda j: (j, 0)),
        out_shape=jax.ShapeDtypeStruct((features, 3 * LANES), BF),
        compiler_params=pltpu.CompilerParams(vmem_limit_bytes=58 << 20),
        cost_estimate=pl.CostEstimate(
            flops=2 * rows * features * 3 * LANES,
            bytes_accessed=2 * features * (2 * rows + 3 * LANES),
            transcendentals=0,
        ),
        name="weight_grads",
    )(x, dy_low, dy_high, d_gate_up, hidden_gated)


def dot(eq, a, b):
    return jnp.einsum(eq, a, b, preferred_element_type=F32)


def shards(tokens, cotangent, route_ids, gates, w_gate, w_up, w_down):
    tok_count, features = tokens.shape
    hidden_dev = w_gate.shape[2]

    mine = jnp.concatenate([w_gate[0].T, w_up[0].T, w_down[0].T], axis=0)
    gathered = lax.all_gather(mine, DP, axis=0, tiled=True)
    n_dp = lax.axis_size(DP)

    ids = route_ids.T
    gates_t = gates.T.astype(F32)
    experts = jnp.arange(EXPERTS, dtype=jnp.int32)
    hits = ids[None] == experts[:, None, None]
    token_hit = jnp.any(hits, axis=1)
    before = (
        jnp.arange(tok_count)[:, None] < jnp.arange(tok_count)[None, :]
    ).astype(BF)
    rank = dot("et,tu->eu", token_hit.astype(BF), before)
    slots = jnp.arange(PAD, dtype=jnp.int32)
    pick = token_hit[:, None, :] & (rank.astype(jnp.int32)[:, None, :] == slots[None, :, None])
    gate_of = jnp.sum(jnp.where(hits, gates_t[None], 0.0), axis=1)
    gate_slots = jnp.sum(jnp.where(pick, gate_of[:, None, :], 0.0), axis=2)
    pick_rows = pick.reshape(EXPERTS * PAD, tok_count).astype(BF)
    tok_slots = dot("ct,td->cd", pick_rows, tokens).astype(BF)
    cot_slots = dot("ct,td->cd", pick_rows, cotangent).astype(BF)
    gate_cols = jnp.broadcast_to(gate_slots.astype(BF).reshape(-1, 1), (EXPERTS * PAD, LANES))
    rows = jnp.concatenate([tok_slots, gate_cols, cot_slots], axis=1)
    rows = rows.reshape(EXPERTS, PAD, -1)
    rows = lax.all_to_all(rows, "ex", split_axis=0, concat_axis=0, tiled=True)
    rows = rows.reshape(EXPERTS * PAD, -1)
    kept = jnp.arange(EXPERTS * CAP)
    keep = (
        (kept // CAP * PAD + kept % CAP)[:, None] == jnp.arange(EXPERTS * PAD)[None, :]
    ).astype(BF)
    wide = features + LANES
    tok_rows = dot("kc,cd->kd", keep, rows[:, :wide]).astype(BF)
    cot_rows = dot("kc,cd->kd", keep, rows[:, wide:]).astype(BF)

    block = EXPERTS * CAP
    tok_half = lax.all_gather(tok_rows, "x", axis=0, tiled=True)
    cot_half = spread(cot_rows, ("zl", "yl"))
    cot_half, gathered = lax.optimization_barrier((cot_half, gathered))
    slot_all = spread(tok_half, ("zl", "yl"))
    cot_low = lax.all_gather(cot_half[:, :SPLIT], "x", axis=0, tiled=True)
    cot_high = lax.all_gather(cot_half[:, SPLIT:], "x", axis=0, tiled=True)
    gathered = gathered.reshape(n_dp, 3, hidden_dev, features)

    def reorder(values):
        v = values.reshape(4, 4, block, values.shape[-1])
        return jnp.swapaxes(v, 0, 1).reshape(values.shape)

    slab = [gathered[:, j].reshape(n_dp * hidden_dev, features) for j in range(3)]
    gate_slab, up_slab, down_slab = slab
    pad = jnp.zeros((LANES, LANES), BF)
    wide_slab = jnp.concatenate(
        [
            jnp.concatenate([gate_slab, pad], axis=1),
            jnp.concatenate([up_slab, pad], axis=1),
            jnp.concatenate([jnp.zeros((LANES, features), BF), jnp.eye(LANES, dtype=BF)], axis=1),
        ],
        axis=0,
    )
    wide_slab = lax.optimization_barrier(wide_slab)
    both = reorder(dot("rd,hd->rh", slot_all, wide_slab))
    pre_gate = both[:, :LANES]
    pre_up = both[:, LANES : 2 * LANES]
    slot_gates = both[:, 2 * LANES :]
    sigmoid_gate = jax.nn.sigmoid(pre_gate)
    activation = pre_gate * sigmoid_gate
    hidden = (activation * pre_up).astype(BF)
    back_proj = dot("rd,hd->rh", cot_low, down_slab[:, :SPLIT]) + dot(
        "rd,hd->rh", cot_high, down_slab[:, SPLIT:]
    )
    score = jnp.sum(hidden.astype(F32) * back_proj, axis=1, keepdims=True).astype(BF)
    scaled = slot_gates * back_proj
    d_gate = (scaled * pre_up * sigmoid_gate * (1.0 + pre_gate * (1.0 - sigmoid_gate))).astype(BF)
    d_up = (scaled * activation).astype(BF)
    hidden_gated = (slot_gates * hidden.astype(F32)).astype(BF)

    left = jnp.concatenate([d_gate, d_up, jnp.broadcast_to(score, d_up.shape)], axis=1)
    back = dot("rh,hd->rd", left, wide_slab).astype(BF)
    grads = weight_grads(
        slot_all, cot_low, cot_high, reorder(left[:, : 2 * LANES]), hidden_gated, features
    )
    grads = lax.psum_scatter(grads, DP, scatter_dimension=0, tiled=True)

    back = back.reshape(8, 2 * block, wide)
    back = lax.all_to_all(back, ("x", "zl"), split_axis=0, concat_axis=0, tiled=True)
    back = back.reshape(HSPLIT * block, wide)
    row = jnp.arange(2 * block)
    target = (row // CAP % EXPERTS * 2 + row // block) * PAD + row % CAP
    fold = (jnp.arange(2 * EXPERTS * PAD)[:, None] == target[None, :]).astype(BF)
    home = dot("ck,kd->cd", jnp.tile(fold, (1, 8)), back).astype(BF)
    home = lax.all_to_all(
        home.reshape(2 * EXPERTS, PAD, wide), ("ex", "yl"), split_axis=0, concat_axis=0, tiled=True
    ).reshape(2 * EXPERTS * PAD, wide)
    pick_home = jnp.broadcast_to(pick[:, None], (EXPERTS, 2, PAD, tok_count))
    pick_home = pick_home.reshape(2 * EXPERTS * PAD, tok_count).astype(BF)
    token_grad = dot("ct,cd->td", pick_home, home[:, :features]).astype(BF)
    score_slots = jnp.sum(
        home[:, features : features + 1].astype(F32).reshape(EXPERTS, 2, PAD, 1), axis=1
    )
    score_token = jnp.sum(jnp.where(pick, score_slots, 0.0), axis=1)
    gate_grad = jnp.sum(jnp.where(hits, score_token[:, None, :], 0.0), axis=0).T

    token_grad, gate_grad, grads = lax.optimization_barrier((token_grad, gate_grad, grads))
    grads = [grads[None, :, LANES * j : LANES * (j + 1)].astype(F32) for j in range(3)]

    start = lax.axis_index(DP) * (features // n_dp)
    relaid = [
        lax.dynamic_slice_in_dim(w, start, features // n_dp, axis=1).T[None] for w in slab
    ]
    return (*relaid, *grads, token_grad, gate_grad)


def solution(mesh):
    fine = Mesh(
        mesh.devices.reshape(4, 2, 4, 2, 4, 2), ("yh", "core", "ex", "zl", "x", "yl")
    )
    expert = ("ex", "zl", "x", "yl")
    rows = P(DP + expert, None)
    weights = P(expert, None, DP)
    laid = P(expert, DP, None)
    return jax.shard_map(
        shards,
        mesh=fine,
        in_specs=(rows,) * 4 + (weights,) * 3,
        out_specs=(laid,) * 6 + (rows,) * 2,
        check_vma=False,
    )
```

```python
import jax
import jax.numpy as jnp
from jax import lax
from jax.experimental import pallas as pl
from jax.experimental.pallas import tpu as pltpu
from jax.sharding import Mesh
from jax.sharding import PartitionSpec as P

HSPLIT = 16
CAP = 6
PAD = 8
EXPERTS = 4
LANES = 128
CHUNK = 512
SPLIT = 2560
DP = ("yh", "core")
BF = jnp.bfloat16
F32 = jnp.float32


def spread(block, axes):
    count = lax.axis_size(axes)
    copies = jnp.broadcast_to(block[None], (count,) + block.shape)
    got = lax.all_to_all(copies, axes, split_axis=0, concat_axis=0, tiled=True)
    return got.reshape((count * block.shape[0],) + block.shape[1:])


def weight_grads(x, dy_low, dy_high, d_gate_up, hidden_gated, features):
    rows = x.shape[0]
    low = dy_low.shape[1] // CHUNK
    over_rows = (((0,), (0,)), ((), ()))

    def kernel(x_ref, low_ref, high_ref, d_ref, h_ref, o_ref):
        def product(a, b):
            return lax.dot_general(a, b, over_rows, preferred_element_type=F32).astype(BF)

        o_ref[:, : 2 * LANES] = product(x_ref[...], d_ref[...])

        @pl.when(pl.program_id(0) < low)
        def _():
            o_ref[:, 2 * LANES :] = product(low_ref[...], h_ref[...])

        @pl.when(pl.program_id(0) >= low)
        def _():
            o_ref[:, 2 * LANES :] = product(high_ref[...], h_ref[...])

    return pl.pallas_call(
        kernel,
        grid=(features // CHUNK,),
        in_specs=[
            pl.BlockSpec((rows, CHUNK), lambda j: (0, j)),
            pl.BlockSpec((rows, CHUNK), lambda j: (0, jnp.minimum(j, low - 1))),
            pl.BlockSpec((rows, CHUNK), lambda j: (0, jnp.maximum(j - low, 0))),
            pl.BlockSpec((rows, 2 * LANES), lambda j: (0, 0)),
            pl.BlockSpec((rows, LANES), lambda j: (0, 0)),
        ],
        out_specs=pl.BlockSpec((CHUNK, 3 * LANES), lambda j: (j, 0)),
        out_shape=jax.ShapeDtypeStruct((features, 3 * LANES), BF),
        compiler_params=pltpu.CompilerParams(vmem_limit_bytes=52 << 20),
        cost_estimate=pl.CostEstimate(
            flops=2 * rows * features * 3 * LANES,
            bytes_accessed=2 * features * (2 * rows + 3 * LANES),
            transcendentals=0,
        ),
        name="weight_grads",
    )(x, dy_low, dy_high, d_gate_up, hidden_gated)


def dot(eq, a, b):
    return jnp.einsum(eq, a, b, preferred_element_type=F32)


def shards(tokens, cotangent, route_ids, gates, w_gate, w_up, w_down):
    tok_count, features = tokens.shape
    hidden_dev = w_gate.shape[2]

    mine = jnp.concatenate([w_gate[0].T, w_up[0].T, w_down[0].T], axis=0)
    gathered = lax.all_gather(mine, DP, axis=0, tiled=True)
    n_dp = lax.axis_size(DP)

    ids = route_ids.T
    gates_t = gates.T.astype(F32)
    experts = jnp.arange(EXPERTS, dtype=jnp.int32)
    hits = ids[None] == experts[:, None, None]
    token_hit = jnp.any(hits, axis=1)
    before = (
        jnp.arange(tok_count)[:, None] < jnp.arange(tok_count)[None, :]
    ).astype(BF)
    rank = dot("et,tu->eu", token_hit.astype(BF), before)
    slots = jnp.arange(PAD, dtype=jnp.int32)
    pick = token_hit[:, None, :] & (rank.astype(jnp.int32)[:, None, :] == slots[None, :, None])
    gate_of = jnp.sum(jnp.where(hits, gates_t[None], 0.0), axis=1)
    gate_slots = jnp.sum(jnp.where(pick, gate_of[:, None, :], 0.0), axis=2)
    pick_rows = pick.reshape(EXPERTS * PAD, tok_count).astype(BF)
    tok_slots = dot("ct,td->cd", pick_rows, tokens).astype(BF)
    cot_slots = dot("ct,td->cd", pick_rows, cotangent).astype(BF)
    gate_cols = jnp.broadcast_to(gate_slots.astype(BF).reshape(-1, 1), (EXPERTS * PAD, LANES))
    rows = jnp.concatenate([tok_slots, gate_cols, cot_slots], axis=1)
    rows = rows.reshape(EXPERTS, PAD, -1)
    rows = lax.all_to_all(rows, "ex", split_axis=0, concat_axis=0, tiled=True)
    rows = rows.reshape(EXPERTS * PAD, -1)
    kept = jnp.arange(EXPERTS * CAP)
    keep = (
        (kept // CAP * PAD + kept % CAP)[:, None] == jnp.arange(EXPERTS * PAD)[None, :]
    ).astype(BF)
    wide = features + LANES
    tok_rows = dot("kc,cd->kd", keep, rows[:, :wide]).astype(BF)
    cot_rows = dot("kc,cd->kd", keep, rows[:, wide:]).astype(BF)

    block = EXPERTS * CAP
    tok_half = lax.all_gather(tok_rows, "x", axis=0, tiled=True)
    cot_half = spread(cot_rows, ("zl", "yl"))
    cot_half, gathered = lax.optimization_barrier((cot_half, gathered))
    slot_all = spread(tok_half, ("zl", "yl"))
    cot_low = lax.all_gather(cot_half[:, :SPLIT], "x", axis=0, tiled=True)
    cot_high = lax.all_gather(cot_half[:, SPLIT:], "x", axis=0, tiled=True)
    gathered = gathered.reshape(n_dp, 3, hidden_dev, features)

    def reorder(values):
        v = values.reshape(4, 4, block, values.shape[-1])
        return jnp.swapaxes(v, 0, 1).reshape(values.shape)

    slab = [gathered[:, j].reshape(n_dp * hidden_dev, features) for j in range(3)]
    gate_slab, up_slab, down_slab = slab
    pad = jnp.zeros((LANES, LANES), BF)
    wide_slab = jnp.concatenate(
        [
            jnp.concatenate([gate_slab, pad], axis=1),
            jnp.concatenate([up_slab, pad], axis=1),
            jnp.concatenate([jnp.zeros((LANES, features), BF), jnp.eye(LANES, dtype=BF)], axis=1),
        ],
        axis=0,
    )
    wide_slab = lax.optimization_barrier(wide_slab)
    both = reorder(dot("rd,hd->rh", slot_all, wide_slab))
    pre_gate = both[:, :LANES]
    pre_up = both[:, LANES : 2 * LANES]
    slot_gates = both[:, 2 * LANES :]
    sigmoid_gate = jax.nn.sigmoid(pre_gate)
    activation = pre_gate * sigmoid_gate
    hidden = (activation * pre_up).astype(BF)
    back_proj = dot("rd,hd->rh", cot_low, down_slab[:, :SPLIT]) + dot(
        "rd,hd->rh", cot_high, down_slab[:, SPLIT:]
    )
    score = jnp.sum(hidden.astype(F32) * back_proj, axis=1, keepdims=True).astype(BF)
    scaled = slot_gates * back_proj
    d_gate = (scaled * pre_up * sigmoid_gate * (1.0 + pre_gate * (1.0 - sigmoid_gate))).astype(BF)
    d_up = (scaled * activation).astype(BF)
    hidden_gated = (slot_gates * hidden.astype(F32)).astype(BF)

    left = jnp.concatenate([d_gate, d_up, jnp.broadcast_to(score, d_up.shape)], axis=1)
    back = dot("rh,hd->rd", left, wide_slab).astype(BF)
    grads = weight_grads(
        slot_all, cot_low, cot_high, reorder(left[:, : 2 * LANES]), hidden_gated, features
    )
    grads = lax.psum_scatter(grads, DP, scatter_dimension=0, tiled=True)

    back = back.reshape(8, 2 * block, wide)
    back = lax.all_to_all(back, ("x", "zl"), split_axis=0, concat_axis=0, tiled=True)
    back = back.reshape(HSPLIT * block, wide)
    row = jnp.arange(2 * block)
    target = (row // CAP % EXPERTS * 2 + row // block) * PAD + row % CAP
    fold = (jnp.arange(2 * EXPERTS * PAD)[:, None] == target[None, :]).astype(BF)
    home = dot("ck,kd->cd", jnp.tile(fold, (1, 8)), back).astype(BF)
    home = lax.all_to_all(
        home.reshape(2 * EXPERTS, PAD, wide), ("ex", "yl"), split_axis=0, concat_axis=0, tiled=True
    ).reshape(2 * EXPERTS * PAD, wide)
    pick_home = jnp.broadcast_to(pick[:, None], (EXPERTS, 2, PAD, tok_count))
    pick_home = pick_home.reshape(2 * EXPERTS * PAD, tok_count).astype(BF)
    token_grad = dot("ct,cd->td", pick_home, home[:, :features]).astype(BF)
    score_slots = jnp.sum(
        home[:, features : features + 1].astype(F32).reshape(EXPERTS, 2, PAD, 1), axis=1
    )
    score_token = jnp.sum(jnp.where(pick, score_slots, 0.0), axis=1)
    gate_grad = jnp.sum(jnp.where(hits, score_token[:, None, :], 0.0), axis=0).T

    token_grad, gate_grad, grads = lax.optimization_barrier((token_grad, gate_grad, grads))
    grads = [grads[None, :, LANES * j : LANES * (j + 1)].astype(F32) for j in range(3)]

    start = lax.axis_index(DP) * (features // n_dp)
    relaid = [
        lax.dynamic_slice_in_dim(w, start, features // n_dp, axis=1).T[None] for w in slab
    ]
    return (*relaid, *grads, token_grad, gate_grad)


def solution(mesh):
    fine = Mesh(
        mesh.devices.reshape(4, 2, 4, 2, 4, 2), ("yh", "core", "ex", "zl", "x", "yl")
    )
    expert = ("ex", "zl", "x", "yl")
    rows = P(DP + expert, None)
    weights = P(expert, None, DP)
    laid = P(expert, DP, None)
    return jax.shard_map(
        shards,
        mesh=fine,
        in_specs=(rows,) * 4 + (weights,) * 3,
        out_specs=(laid,) * 6 + (rows,) * 2,
        check_vma=False,
    )
```

```python
import jax
import jax.numpy as jnp
from jax import lax
from jax.experimental import pallas as pl
from jax.experimental.pallas import tpu as pltpu
from jax.sharding import Mesh
from jax.sharding import PartitionSpec as P

HSPLIT = 16
CAP = 6
PAD = 8
EXPERTS = 4
LANES = 128
CHUNK = 512
SPLIT = 2560
DP = ("yh", "core")
BF = jnp.bfloat16
F32 = jnp.float32


def spread(block, axes):
    count = lax.axis_size(axes)
    copies = jnp.broadcast_to(block[None], (count,) + block.shape)
    got = lax.all_to_all(copies, axes, split_axis=0, concat_axis=0, tiled=True)
    return got.reshape((count * block.shape[0],) + block.shape[1:])


def weight_grads(x, dy_low, dy_high, d_gate_up, hidden_gated, features):
    rows = x.shape[0]
    low = dy_low.shape[1] // CHUNK
    over_rows = (((0,), (0,)), ((), ()))

    def kernel(x_ref, low_ref, high_ref, d_ref, h_ref, o_ref):
        def product(a, b):
            return lax.dot_general(a, b, over_rows, preferred_element_type=F32).astype(BF)

        o_ref[:, : 2 * LANES] = product(x_ref[...], d_ref[...])

        @pl.when(pl.program_id(0) < low)
        def _():
            o_ref[:, 2 * LANES :] = product(low_ref[...], h_ref[...])

        @pl.when(pl.program_id(0) >= low)
        def _():
            o_ref[:, 2 * LANES :] = product(high_ref[...], h_ref[...])

    return pl.pallas_call(
        kernel,
        grid=(features // CHUNK,),
        in_specs=[
            pl.BlockSpec((rows, CHUNK), lambda j: (0, j)),
            pl.BlockSpec((rows, CHUNK), lambda j: (0, jnp.minimum(j, low - 1))),
            pl.BlockSpec((rows, CHUNK), lambda j: (0, jnp.maximum(j - low, 0))),
            pl.BlockSpec((rows, 2 * LANES), lambda j: (0, 0)),
            pl.BlockSpec((rows, LANES), lambda j: (0, 0)),
        ],
        out_specs=pl.BlockSpec((CHUNK, 3 * LANES), lambda j: (j, 0)),
        out_shape=jax.ShapeDtypeStruct((features, 3 * LANES), BF),
        compiler_params=pltpu.CompilerParams(vmem_limit_bytes=52 << 20),
        cost_estimate=pl.CostEstimate(
            flops=2 * rows * features * 3 * LANES,
            bytes_accessed=2 * features * (2 * rows + 3 * LANES),
            transcendentals=0,
        ),
        name="weight_grads",
    )(x, dy_low, dy_high, d_gate_up, hidden_gated)


def dot(eq, a, b):
    return jnp.einsum(eq, a, b, preferred_element_type=F32)


def shards(tokens, cotangent, route_ids, gates, w_gate, w_up, w_down):
    tok_count, features = tokens.shape
    hidden_dev = w_gate.shape[2]

    mine = jnp.concatenate([w_gate[0].T, w_up[0].T, w_down[0].T], axis=0)
    gathered = lax.all_gather(mine, DP, axis=0, tiled=True)
    n_dp = lax.axis_size(DP)

    ids = route_ids.T
    gates_t = gates.T.astype(F32)
    experts = jnp.arange(EXPERTS, dtype=jnp.int32)
    hits = ids[None] == experts[:, None, None]
    token_hit = jnp.any(hits, axis=1)
    before = (
        jnp.arange(tok_count)[:, None] < jnp.arange(tok_count)[None, :]
    ).astype(BF)
    rank = dot("et,tu->eu", token_hit.astype(BF), before)
    slots = jnp.arange(PAD, dtype=jnp.int32)
    pick = token_hit[:, None, :] & (rank.astype(jnp.int32)[:, None, :] == slots[None, :, None])
    gate_of = jnp.sum(jnp.where(hits, gates_t[None], 0.0), axis=1)
    gate_slots = jnp.sum(jnp.where(pick, gate_of[:, None, :], 0.0), axis=2)
    pick_rows = pick.reshape(EXPERTS * PAD, tok_count).astype(BF)
    tok_slots = dot("ct,td->cd", pick_rows, tokens).astype(BF)
    cot_slots = dot("ct,td->cd", pick_rows, cotangent).astype(BF)
    gate_cols = jnp.broadcast_to(gate_slots.astype(BF).reshape(-1, 1), (EXPERTS * PAD, LANES))
    rows = jnp.concatenate([tok_slots, gate_cols, cot_slots], axis=1)
    rows = rows.reshape(EXPERTS, PAD, -1)
    rows = lax.all_to_all(rows, "ex", split_axis=0, concat_axis=0, tiled=True)
    rows = rows.reshape(EXPERTS * PAD, -1)
    kept = jnp.arange(EXPERTS * CAP)
    keep = (
        (kept // CAP * PAD + kept % CAP)[:, None] == jnp.arange(EXPERTS * PAD)[None, :]
    ).astype(BF)
    wide = features + LANES
    tok_rows = dot("kc,cd->kd", keep, rows[:, :wide]).astype(BF)
    cot_rows = dot("kc,cd->kd", keep, rows[:, wide:]).astype(BF)

    block = EXPERTS * CAP
    tok_half = lax.all_gather(tok_rows, "x", axis=0, tiled=True)
    cot_half = spread(cot_rows, ("zl", "yl"))
    cot_half, gathered = lax.optimization_barrier((cot_half, gathered))
    slot_all = spread(tok_half, ("zl", "yl"))
    cot_low = lax.all_gather(cot_half[:, :SPLIT], "x", axis=0, tiled=True)
    cot_high = lax.all_gather(cot_half[:, SPLIT:], "x", axis=0, tiled=True)
    gathered = gathered.reshape(n_dp, 3, hidden_dev, features)

    def reorder(values):
        v = values.reshape(4, 4, block, values.shape[-1])
        return jnp.swapaxes(v, 0, 1).reshape(values.shape)

    slab = [gathered[:, j].reshape(n_dp * hidden_dev, features) for j in range(3)]
    gate_slab, up_slab, down_slab = slab
    pad = jnp.zeros((LANES, LANES), BF)
    wide_slab = jnp.concatenate(
        [
            jnp.concatenate([gate_slab, pad], axis=1),
            jnp.concatenate([up_slab, pad], axis=1),
            jnp.concatenate([jnp.zeros((LANES, features), BF), jnp.eye(LANES, dtype=BF)], axis=1),
        ],
        axis=0,
    )
    wide_slab = lax.optimization_barrier(wide_slab)
    both = reorder(dot("rd,hd->rh", slot_all, wide_slab[: 2 * LANES]))
    pre_gate = both[:, :LANES]
    pre_up = both[:, LANES:]
    slot_gates = reorder(slot_all[:, features:]).astype(F32)
    sigmoid_gate = jax.nn.sigmoid(pre_gate)
    activation = pre_gate * sigmoid_gate
    hidden = (activation * pre_up).astype(BF)
    back_proj = dot("rd,hd->rh", cot_low, down_slab[:, :SPLIT]) + dot(
        "rd,hd->rh", cot_high, down_slab[:, SPLIT:]
    )
    score = jnp.sum(hidden.astype(F32) * back_proj, axis=1, keepdims=True).astype(BF)
    scaled = slot_gates * back_proj
    d_gate = (scaled * pre_up * sigmoid_gate * (1.0 + pre_gate * (1.0 - sigmoid_gate))).astype(BF)
    d_up = (scaled * activation).astype(BF)
    hidden_gated = (slot_gates * hidden.astype(F32)).astype(BF)

    left = jnp.concatenate([d_gate, d_up, jnp.broadcast_to(score, d_up.shape)], axis=1)
    back = dot("rh,hd->rd", left, wide_slab).astype(BF)
    grads = weight_grads(
        slot_all, cot_low, cot_high, reorder(left[:, : 2 * LANES]), hidden_gated, features
    )
    grads = lax.psum_scatter(grads, DP, scatter_dimension=0, tiled=True)

    back = back.reshape(8, 2 * block, wide)
    back = lax.all_to_all(back, ("x", "zl"), split_axis=0, concat_axis=0, tiled=True)
    back = back.reshape(HSPLIT * block, wide)
    row = jnp.arange(2 * block)
    target = (row // CAP % EXPERTS * 2 + row // block) * PAD + row % CAP
    fold = (jnp.arange(2 * EXPERTS * PAD)[:, None] == target[None, :]).astype(BF)
    home = dot("ck,kd->cd", jnp.tile(fold, (1, 8)), back).astype(BF)
    home = lax.all_to_all(
        home.reshape(2 * EXPERTS, PAD, wide), ("ex", "yl"), split_axis=0, concat_axis=0, tiled=True
    ).reshape(2 * EXPERTS * PAD, wide)
    pick_home = jnp.broadcast_to(pick[:, None], (EXPERTS, 2, PAD, tok_count))
    pick_home = pick_home.reshape(2 * EXPERTS * PAD, tok_count).astype(BF)
    token_grad = dot("ct,cd->td", pick_home, home[:, :features]).astype(BF)
    score_slots = jnp.sum(
        home[:, features : features + 1].astype(F32).reshape(EXPERTS, 2, PAD, 1), axis=1
    )
    score_token = jnp.sum(jnp.where(pick, score_slots, 0.0), axis=1)
    gate_grad = jnp.sum(jnp.where(hits, score_token[:, None, :], 0.0), axis=0).T

    token_grad, gate_grad, grads = lax.optimization_barrier((token_grad, gate_grad, grads))
    grads = [grads[None, :, LANES * j : LANES * (j + 1)].astype(F32) for j in range(3)]

    start = lax.axis_index(DP) * (features // n_dp)
    relaid = [
        lax.dynamic_slice_in_dim(w, start, features // n_dp, axis=1).T[None] for w in slab
    ]
    return (*relaid, *grads, token_grad, gate_grad)


def solution(mesh):
    fine = Mesh(
        mesh.devices.reshape(4, 2, 4, 2, 4, 2), ("yh", "core", "ex", "zl", "x", "yl")
    )
    expert = ("ex", "zl", "x", "yl")
    rows = P(DP + expert, None)
    weights = P(expert, None, DP)
    laid = P(expert, DP, None)
    return jax.shard_map(
        shards,
        mesh=fine,
        in_specs=(rows,) * 4 + (weights,) * 3,
        out_specs=(laid,) * 6 + (rows,) * 2,
        check_vma=False,
    )
```
